32 devices in a mesh: head: 4 (over y, x), frame: 8 (over z, core).
Axes of the slice: x: 2, y: 2, z: 4, core: 2. Of those that a mesh axis runs over, the one named last changes fastest.
Arguments:
- query_tok: bfloat16 [6144, 3072], P('frame', 'head'), may hold values from -200 to 200
- key_tok: bfloat16 [6144, 3072], P('frame', 'head'), may hold values from -8 to 8
- value_tok: bfloat16 [6144, 3072], P('frame', 'head'), may hold values from -6 to 6
- head_span: int32 [24], P('head'), may hold values from 0 to 3
- out_weight: bfloat16 [3072, 3072], P('head'), may hold values from -0.109375 to 0.109375
Outputs:
- projected: bfloat16 [6144, 3072], P('frame', 'head')
The draws below stay inside these ranges and needn't reach their ends.
All inputs are finite; a program needn't handle non-finite values.
Results may differ from the reference program's by a relative error of at most 0.012.
Values may be sent and summed in bfloat16 or wider, within the bound.
No kernel may reach another device: no remote copies, remote signals or barrier semaphores. Data moves between devices by JAX's collectives and lax.ppermute only.
A program may use at most 128 MiB of HBM per device.

```python
import jax
import jax.numpy as jnp
from jax import lax

HEADS = 24
HD = 128
D = 3072
FRAME_TOK = 384
FRAMES = 16
TOKENS = 6144
N_HEAD = 4


def shared_keys(key):
    return jnp.clip(jax.random.normal(jax.random.fold_in(key, 11), (TOKENS, HEADS * HD), jnp.float32), -8.0, 8.0)


def draw_key_tok(key, part):
    return shared_keys(key).astype(jnp.bfloat16)


def draw_query_tok(key, part):
    base = jnp.clip(jax.random.normal(jax.random.fold_in(key, 12), (TOKENS, HEADS * HD), jnp.float32), -6.0, 6.0)
    return base.astype(jnp.bfloat16)


def touch_ends(entries, own_key, smallest, largest):
    spot = [jax.random.randint(jax.random.fold_in(own_key, axis), (), 0, length) for axis, length in enumerate(entries.shape)]
    widest = entries.shape.index(max(entries.shape))
    next_to = spot[:widest] + [(spot[widest] + 1) % entries.shape[widest]] + spot[widest + 1:]
    return entries.at[tuple(spot)].set(smallest).at[tuple(next_to)].set(largest)


def block_scale(rng, shape, shards, smallest, largest):
    def one(dim, parts):
        steps = jax.random.uniform(jax.random.fold_in(jax.random.fold_in(rng, 6), dim), (parts,), jnp.float32, smallest / len(shards), largest / len(shards))
        return jnp.repeat(jnp.exp(steps), shape[dim] // parts).reshape((-1,) + (1,) * (len(shape) - dim - 1))

    loudness = one(*shards[0])
    for cut in shards[1:]:
        loudness = loudness * one(*cut)
    return loudness


def noise(stream_key, dims, spread, bound, split=(), kind=jnp.bfloat16):
    factor_of = block_scale(stream_key, dims, split, -0.22, 0.18) if split else 1.0
    values = jax.random.normal(stream_key, dims, jnp.float32) * spread * factor_of
    return jnp.minimum(jnp.maximum(values, -bound), bound).astype(kind)


def setup_inputs(seed: int = 0) -> dict:
    key_list = jax.random.split(jax.random.key(seed), 6)
    query_tok = draw_query_tok(jax.random.fold_in(key_list[5], 71), 0)
    key_tok = draw_key_tok(jax.random.fold_in(key_list[5], 71), 0)
    value_tok = noise(key_list[2], (TOKENS, HEADS * HD), 1.0, 6.0, ((0, 8), (1, 4)))
    head_span = touch_ends(jax.random.randint(key_list[3], (HEADS,), 0, 4), jax.random.fold_in(key_list[3], 1), 0, 3).astype(jnp.int32)
    out_weight = noise(key_list[4], (HEADS * HD, D), (HEADS * HD) ** -0.5, 0.109375, ((0, 4),))
    return dict(query_tok=query_tok, key_tok=key_tok, value_tok=value_tok, head_span=head_span, out_weight=out_weight)


def attend(query_frame, key_rows, value_rows, frame_pos, head_span):
    scale = 1.0 / (HD ** 0.5)
    scores = jnp.einsum("qhd,khd->hqk", query_frame.astype(jnp.float32), key_rows.astype(jnp.float32)) * scale
    offsets = jnp.arange(7, dtype=jnp.int32) - 3
    allowed = (jnp.abs(offsets)[None, :] <= head_span[:, None]) & (frame_pos + offsets >= 0)[None, :] & (frame_pos + offsets < FRAMES)[None, :]
    visible = jnp.repeat(allowed, FRAME_TOK, axis=1)[:, None, :]
    scores = jnp.where(visible, scores, -1e30)
    rowmax = jnp.max(scores, axis=2, keepdims=True)
    weights = jnp.where(visible, jnp.exp(scores - rowmax), 0.0)
    total = jnp.sum(weights, axis=2)
    probs = weights.astype(jnp.bfloat16)
    mixed = jnp.einsum("hqk,khd->qhd", probs.astype(jnp.float32), value_rows.astype(jnp.float32))
    return (mixed / jnp.transpose(total)[:, :, None]).astype(jnp.bfloat16)


def reference(query_tok, key_tok, value_tok, head_span, out_weight):
    query_all = query_tok.reshape(FRAMES, FRAME_TOK, HEADS, HD)
    widths = ((3, 3), (0, 0), (0, 0), (0, 0))
    key_pad = jnp.pad(key_tok.reshape(FRAMES, FRAME_TOK, HEADS, HD), widths)
    value_pad = jnp.pad(value_tok.reshape(FRAMES, FRAME_TOK, HEADS, HD), widths)

    def one_frame(frame_pos):
        key_rows = lax.dynamic_slice_in_dim(key_pad, frame_pos, 7, 0).reshape(7 * FRAME_TOK, HEADS, HD)
        value_rows = lax.dynamic_slice_in_dim(value_pad, frame_pos, 7, 0).reshape(7 * FRAME_TOK, HEADS, HD)
        query_frame = lax.dynamic_index_in_dim(query_all, frame_pos, 0, keepdims=False)
        return attend(query_frame, key_rows, value_rows, frame_pos, head_span)

    attended = lax.map(one_frame, jnp.arange(FRAMES, dtype=jnp.int32)).reshape(TOKENS, HEADS * HD)
    group = HEADS * HD // N_HEAD
    summed = jnp.zeros((TOKENS, D), jnp.float32)
    for index in range(N_HEAD):
        partial_value = jnp.dot(attended[:, index * group:(index + 1) * group], out_weight[index * group:(index + 1) * group], preferred_element_type=jnp.float32).astype(jnp.bfloat16)
        partial_value = lax.optimization_barrier(partial_value)
        summed = summed + partial_value.astype(jnp.float32)
    return summed.astype(jnp.bfloat16)
```

```python
import jax
import jax.numpy as jnp
from jax import lax
from jax.experimental import pallas as pl
from jax.experimental.pallas import tpu as pltpu
from jax.sharding import PartitionSpec as P

HD = 128
FRAME_TOK = 384
LOG2E = 1.4426950408889634
F32 = jnp.float32
BF16 = jnp.bfloat16
VMEM_LIMIT = 24 << 20


def params(grid_len):
    return pltpu.CompilerParams(
        dimension_semantics=("arbitrary",) * grid_len, vmem_limit_bytes=VMEM_LIMIT
    )


def pack_frames(table, key_tok, value_tok):
    width = key_tok.shape[1]

    def kernel(table_ref, key_e, value_e, key_i, value_i, out_e, out_i):
        out_e[:FRAME_TOK, :] = key_e[...]
        out_e[FRAME_TOK:, :] = value_e[...]
        out_i[:FRAME_TOK, :] = key_i[...]
        out_i[FRAME_TOK:, :] = value_i[...]

    edge = pl.BlockSpec((FRAME_TOK, HD), lambda h, t: (t[0], h))
    inner = pl.BlockSpec((FRAME_TOK, HD), lambda h, t: (1 - t[0], h))
    out = pl.BlockSpec((2 * FRAME_TOK, HD), lambda h, t: (0, h))
    shape = jax.ShapeDtypeStruct((2 * FRAME_TOK, width), BF16)
    return pl.pallas_call(
        kernel,
        out_shape=(shape, shape),
        grid_spec=pltpu.PrefetchScalarGridSpec(
            num_scalar_prefetch=1,
            grid=(width // HD,),
            in_specs=[edge, edge, inner, inner],
            out_specs=(out, out),
        ),
        compiler_params=params(1),
        name="pack_frames",
    )(table, key_tok, value_tok, key_tok, value_tok)


def attend_step(name, table, query_tok, sources, roles, first, last):
    heads = query_tok.shape[1] // HD
    names = list(roles)
    scale = LOG2E / HD**0.5

    def kernel(table_ref, *refs):
        refs = list(refs)
        queries = {role: refs.pop(0) for role in names}
        loaded = [(refs.pop(0), refs.pop(0)) for _ in sources]
        olds = {} if first else {role: [refs.pop(0) for _ in range(3)] for role in names}
        outs = {role: [refs.pop(0) for _ in range(1 if last else 3)] for role in names}
        span = table_ref[3 + pl.program_id(0)]

        def emit(role, acc, total, top):
            if last:
                outs[role][0][...] = (acc / total).astype(BF16)
            else:
                outs[role][0][...] = acc
                outs[role][1][...] = total
                outs[role][2][...] = top

        def update(role, picked):
            if not picked:
                emit(role, *(ref[...] for ref in olds[role]))
                return
            keys = jnp.concatenate([loaded[i][0][...] for i in picked], axis=0)
            values = jnp.concatenate([loaded[i][1][...] for i in picked], axis=0)
            values = jnp.concatenate([values, jnp.ones_like(values)], axis=1)
            scores = lax.dot_general(
                queries[role][...], keys, (((1,), (1,)), ((), ())), preferred_element_type=F32
            )
            top = jnp.max(scores, axis=1, keepdims=True)
            if not first:
                old_acc, old_total, old_top = (ref[...] for ref in olds[role])
                top = jnp.maximum(top, old_top[:, :1])
            weights = jnp.exp2((scores - top) * scale).astype(BF16)
            mixed = jnp.dot(weights, values, preferred_element_type=F32)
            acc, total = mixed[:, :HD], mixed[:, HD:]
            if not first:
                fade = jnp.exp2((old_top - top) * scale)
                acc = old_acc * fade + acc
                total = old_total * fade + total
            emit(role, acc, total, jnp.broadcast_to(top, (FRAME_TOK, HD)))

        for role in names:
            entries = roles[role][1]
            if first:
                spans = {}
                for limit in range(4):
                    picked = tuple(i for i, distance, _ in entries if distance <= limit)
                    spans.setdefault(picked, []).append(limit)
                for picked, limits in spans.items():
                    pl.when((span >= limits[0]) & (span <= limits[-1]))(
                        lambda role=role, picked=picked: update(role, picked)
                    )
            else:
                mask = sum(
                    jnp.where((span >= distance) & (table_ref[slot] > 0), 1 << bit, 0)
                    for bit, (_, distance, slot) in enumerate(entries)
                )
                for value in range(1 << len(entries)):
                    picked = tuple(e[0] for bit, e in enumerate(entries) if value >> bit & 1)
                    pl.when(mask == value)(lambda role=role, picked=picked: update(role, picked))

    query_spec = {
        "E": pl.BlockSpec((FRAME_TOK, HD), lambda h, t: (t[0], h)),
        "I": pl.BlockSpec((FRAME_TOK, HD), lambda h, t: (1 - t[0], h)),
    }
    key_spec = pl.BlockSpec((FRAME_TOK, HD), lambda h, t: (0, h))
    value_spec = pl.BlockSpec((FRAME_TOK, HD), lambda h, t: (1, h))
    column = pl.BlockSpec((FRAME_TOK, HD), lambda h, t: (0, h))
    in_specs = [query_spec[role] for role in names] + [key_spec, value_spec] * len(sources)
    operands = [query_tok] * len(names)
    for source in sources:
        operands += [source, source]
    if not first:
        for role in names:
            operands += list(roles[role][0])
            in_specs += [column] * 3
    per_role = 1 if last else 3
    shape = jax.ShapeDtypeStruct((FRAME_TOK, heads * HD), BF16 if last else F32)
    count = per_role * len(names)
    out = pl.pallas_call(
        kernel,
        out_shape=(shape,) * count,
        grid_spec=pltpu.PrefetchScalarGridSpec(
            num_scalar_prefetch=1, grid=(heads,), in_specs=in_specs, out_specs=(column,) * count
        ),
        compiler_params=params(1),
        name=name,
    )(table, *operands)
    return {role: out[i * per_role : (i + 1) * per_role] for i, role in enumerate(names)}


def project(name, attended, part, parts, out_weight, columns, received, width, into=None):
    rows = attended.shape[0] // parts
    depth = attended.shape[1]
    count = columns.shape[0]
    place = jnp.zeros((1,), jnp.int32) if into is None else into[0].reshape(1)
    positions = jnp.asarray([p for _, spots in received for p in spots], jnp.int32)
    scalars = jnp.concatenate([place, columns, positions])

    def kernel(scalars_ref, left, right, *rest):
        out = rest[-1]
        sums = jnp.dot(left[...], right[...], preferred_element_type=F32)
        for ref in rest[: len(received)]:
            sums = sums + ref[...].astype(F32)
        out[...] = sums.astype(BF16)

    in_specs = [
        pl.BlockSpec((rows, depth), lambda i, s: (part, 0)),
        pl.BlockSpec((depth, width), lambda i, s: (0, s[1 + i])),
    ]
    operands = [attended, out_weight]
    for index, (array, _) in enumerate(received):
        in_specs.append(
            pl.BlockSpec((rows, width), lambda i, s, index=index: (0, s[1 + count * (1 + index) + i]))
        )
        operands.append(array)
    aliases = {}
    if into is None:
        out_shape = jax.ShapeDtypeStruct((rows, count * width), BF16)
        out_spec = pl.BlockSpec((rows, width), lambda i, s: (0, i))
    else:
        out_shape = jax.ShapeDtypeStruct((into[1] * rows, width), BF16)
        out_spec = pl.BlockSpec((rows, width), lambda i, s: (s[0], 0))
        if into[2] is not None:
            in_specs.append(pl.BlockSpec(memory_space=pl.ANY))
            operands.append(into[2])
            aliases = {len(operands): 0}
    return pl.pallas_call(
        kernel,
        out_shape=out_shape,
        grid_spec=pltpu.PrefetchScalarGridSpec(
            num_scalar_prefetch=1, grid=(count,), in_specs=in_specs, out_specs=out_spec
        ),
        input_output_aliases=aliases,
        compiler_params=params(1),
        name=name,
    )(scalars, *operands)


def body(query_tok, key_tok, value_tok, head_span, out_weight):
    frames = lax.axis_size("frame")
    groups = lax.axis_size("head")
    local_frames = key_tok.shape[0] // FRAME_TOK
    bits = groups.bit_length() - 1
    assert local_frames == 2 and frames % 2 == 0 and groups == 1 << bits and FRAME_TOK % bits == 0
    width = out_weight.shape[1] // groups
    seat = lax.axis_index("frame")
    group = lax.axis_index("head")
    parity = seat % 2
    link = jnp.where(parity == 0, seat > 0, seat < frames - 1)
    far_link = jnp.where(parity == 0, seat < frames - 2, seat > 1)
    table = jnp.concatenate(
        [jnp.stack([parity, link, far_link]).astype(jnp.int32), head_span.astype(jnp.int32)]
    )

    def swap(value):
        return lax.ppermute(value, "frame", [(i, i ^ 1) for i in range(frames)])

    def across(value):
        pairs = [(i, i + 1) for i in range(1, frames - 1, 2)]
        return lax.ppermute(value, "frame", pairs + [(b, a) for a, b in pairs])

    edge, inner = pack_frames(table, key_tok, value_tok)
    near = across(edge)
    partner_inner = swap(inner)
    partner_edge = swap(edge)
    second = across(inner)
    third = across(partner_inner)
    state = attend_step(
        "attend_chip",
        table,
        query_tok,
        [edge, inner, partner_inner, partner_edge],
        {
            "E": (None, [(0, 0, None), (1, 1, None), (2, 2, None), (3, 3, None)]),
            "I": (None, [(1, 0, None), (0, 1, None), (2, 1, None), (3, 2, None)]),
        },
        True,
        False,
    )
    beyond = swap(near)
    state = attend_step(
        "attend_near",
        table,
        query_tok,
        [near, beyond],
        {"E": (state["E"], [(0, 1, 1)]), "I": (state["I"], [(0, 2, 1), (1, 3, 2)])},
        False,
        False,
    )
    attended_i = attend_step(
        "attend_inner", table, query_tok, [second], {"I": (state["I"], [(0, 3, 1)])}, False, True
    )["I"][0]
    attended_e = attend_step(
        "attend_edge",
        table,
        query_tok,
        [second, third],
        {"E": (state["E"], [(0, 2, 1), (1, 3, 1)])},
        False,
        True,
    )["E"][0]

    def exchange(value, bit):
        return lax.ppermute(value, "head", [(i, i ^ (1 << bit)) for i in range(groups)])

    result = None
    for name, attended, frame_index in (("inner", attended_i, 1 - parity), ("edge", attended_e, parity)):
        held = [list(range(groups)) for _ in range(bits)]
        received = [[] for _ in range(bits)]

        def gathered(part, slots):
            return [(array, [kept.index(s) for s in slots]) for array, kept in received[part]]

        for stage in range(bits):
            for part in range(bits):
                bit = (part + stage) % bits
                sent = [s for s in held[part] if s >> bit & 1]
                kept = [s for s in held[part] if not s >> bit & 1]
                terms = project(
                    f"project_{name}_{stage}_{part}",
                    attended,
                    part,
                    bits,
                    out_weight,
                    group ^ jnp.asarray(sent, jnp.int32),
                    gathered(part, sent),
                    width,
                )
                received[part].append((exchange(terms, bit), kept))
                held[part] = kept
        for part in range(bits):
            result = project(
                f"project_{name}_own_{part}",
                attended,
                part,
                bits,
                out_weight,
                group.reshape(1),
                gathered(part, [0]),
                width,
                (frame_index * bits + part, local_frames * bits, result),
            )
    return result


def solution(mesh):
    return jax.shard_map(
        body,
        mesh=mesh,
        in_specs=(
            P("frame", "head"),
            P("frame", "head"),
            P("frame", "head"),
            P("head"),
            P("head", None),
        ),
        out_specs=P("frame", "head"),
        check_vma=False,
    )
```

```python
import jax
import jax.numpy as jnp
from jax import lax
from jax.experimental import pallas as pl
from jax.experimental.pallas import tpu as pltpu
from jax.sharding import PartitionSpec as P


HD = 128
FRAME_TOK = 384
LOG2E = 1.4426950408889634
F32 = jnp.float32
BF16 = jnp.bfloat16
VMEM_LIMIT = 16 << 20


def params():
    return pltpu.CompilerParams(vmem_limit_bytes=VMEM_LIMIT)


VMEM = pl.BlockSpec(memory_space=pltpu.VMEM)
SMEM = pl.BlockSpec(memory_space=pltpu.SMEM)
HBM = pl.BlockSpec(memory_space=pltpu.HBM)


def pack_frames(key_tok, value_tok):
    width = key_tok.shape[1]

    def kernel(key, value, out_e, out_i, sems):
        parity = lax.axis_index("frame") % 2
        copies = []
        for out, frame in ((out_e, parity), (out_i, 1 - parity)):
            for place, source in enumerate((key, value)):
                copies.append(
                    pltpu.make_async_copy(
                        source.at[pl.ds(pl.multiple_of(frame * FRAME_TOK, FRAME_TOK), FRAME_TOK)],
                        out.at[pl.ds(place * FRAME_TOK, FRAME_TOK)],
                        sems.at[len(copies)],
                    )
                )
        for copy in copies:
            copy.start()
        for copy in copies:
            copy.wait()

    shape = jax.ShapeDtypeStruct((2 * FRAME_TOK, width), BF16)
    return pl.pallas_call(
        kernel,
        out_shape=(shape, shape),
        in_specs=[HBM, HBM],
        out_specs=(VMEM, VMEM),
        scratch_shapes=[pltpu.SemaphoreType.DMA((4,))],
        compiler_params=params(),
        name="pack_frames",
    )(key_tok, value_tok)


def attend_step(table, query_tok, sources, roles, first, last):
    heads = query_tok.shape[1] // HD
    names = list(roles)
    scale = LOG2E / HD**0.5
    per_role = 1 if last else 3

    def kernel(table_ref, query, *refs):
        refs = list(refs)
        loaded = [refs.pop(0) for _ in sources]
        olds = {} if first else {role: [refs.pop(0) for _ in range(3)] for role in names}
        outs = {role: [refs.pop(0) for _ in range(per_role)] for role in names}
        parity = table_ref[0]
        starts = {"E": parity * FRAME_TOK, "I": (1 - parity) * FRAME_TOK}

        def one_head(head, carry):
            column = pl.ds(pl.multiple_of(head * HD, HD), HD)
            span = table_ref[3 + head]

            def emit(role, acc, total, top):
                if last:
                    outs[role][0][:, column] = (acc / total).astype(BF16)
                else:
                    outs[role][0][:, column] = acc
                    outs[role][1][:, column] = total
                    outs[role][2][:, column] = jnp.broadcast_to(top, (FRAME_TOK, HD))

            def update(role, picked):
                if not picked:
                    if last:
                        emit(role, *(ref[:, column] for ref in olds[role]))
                    return
                keys = jnp.concatenate([loaded[i][:FRAME_TOK, column] for i in picked], axis=0)
                values = jnp.concatenate([loaded[i][FRAME_TOK:, column] for i in picked], axis=0)
                values = jnp.concatenate([values, jnp.ones_like(values)], axis=1)
                rows = pl.ds(pl.multiple_of(starts[role], FRAME_TOK), FRAME_TOK)
                scores = lax.dot_general(
                    query[rows, column], keys, (((1,), (1,)), ((), ())), preferred_element_type=F32
                )
                top = jnp.max(scores, axis=1, keepdims=True)
                if not first:
                    old_acc, old_total, old_top = (ref[:, column] for ref in olds[role])
                    top = jnp.maximum(top, old_top[:, :1])
                weights = jnp.exp2((scores - top) * scale).astype(BF16)
                mixed = jnp.dot(weights, values, preferred_element_type=F32)
                acc, total = mixed[:, :HD], mixed[:, HD:]
                if not first:
                    fade = jnp.exp2((old_top - top) * scale)
                    acc = old_acc * fade + acc
                    total = old_total * fade + total
                emit(role, acc, total, top)

            if first:
                for limit in range(4):

                    def both(limit=limit):
                        for role in names:
                            update(role, [i for i, distance, _ in roles[role][1] if distance <= limit])

                    pl.when(span == limit)(both)
            else:
                for role in names:
                    entries = roles[role][1]
                    mask = sum(
                        jnp.where((span >= distance) & (table_ref[slot] > 0), 1 << bit, 0)
                        for bit, (_, distance, slot) in enumerate(entries)
                    )
                    for value in range(1 << len(entries)):
                        picked = [e[0] for bit, e in enumerate(entries) if value >> bit & 1]
                        if picked or last:
                            pl.when(mask == value)(lambda role=role, picked=picked: update(role, picked))
            return carry

        lax.fori_loop(0, heads, one_head, 0)

    operands = [table, query_tok, *sources]
    aliases = {}
    if not first:
        for index, role in enumerate(names):
            if not last:
                aliases.update({len(operands) + i: 3 * index + i for i in range(3)})
            operands += list(roles[role][0])
    shape = jax.ShapeDtypeStruct((FRAME_TOK, heads * HD), BF16 if last else F32)
    count = per_role * len(names)
    out = pl.pallas_call(
        kernel,
        out_shape=(shape,) * count,
        in_specs=[SMEM] + [VMEM] * (len(operands) - 1),
        out_specs=(VMEM,) * count,
        input_output_aliases=aliases,
        compiler_params=params(),
    )(*operands)
    return {role: out[i * per_role : (i + 1) * per_role] for i, role in enumerate(names)}


def project(attended, part, parts, out_weight, slots, received):
    groups = lax.axis_size("head")
    width = out_weight.shape[1] // groups
    rows = attended.shape[0] // parts

    def kernel(left, right, *rest):
        out = rest[-1]
        group = lax.axis_index("head")
        for index, slot in enumerate(slots):
            column = pl.ds(pl.multiple_of((group ^ slot) * width, width), width)
            sums = jnp.dot(
                left[part * rows : (part + 1) * rows, :], right[:, column], preferred_element_type=F32
            )
            for ref, (_, spots) in zip(rest, received):
                sums = sums + ref[:, spots[index] * width : (spots[index] + 1) * width].astype(F32)
            out[:, index * width : (index + 1) * width] = sums.astype(BF16)

    return pl.pallas_call(
        kernel,
        out_shape=jax.ShapeDtypeStruct((rows, len(slots) * width), BF16),
        in_specs=[VMEM] * (2 + len(received)),
        out_specs=VMEM,
        compiler_params=params(),
    )(attended, out_weight, *(array for array, _ in received))


def finish(attended, parts, out_weight, received, is_edge, frames_here, into):
    groups = lax.axis_size("head")
    width = out_weight.shape[1] // groups
    rows = FRAME_TOK // parts
    flat = [(array, spots[0], part) for part in range(parts) for array, spots in received[part]]

    def kernel(left, right, *rest):
        out, buffer, sems = rest[-3:]
        group = lax.axis_index("head")
        parity = lax.axis_index("frame") % 2
        frame = parity if is_edge else 1 - parity
        column = pl.ds(pl.multiple_of(group * width, width), width)
        copies = []
        for part in range(parts):
            span = slice(part * rows, (part + 1) * rows)
            sums = jnp.dot(left[span, :], right[:, column], preferred_element_type=F32)
            for ref, (_, spot, owner) in zip(rest, flat):
                if owner == part:
                    sums = sums + ref[:, spot * width : (spot + 1) * width].astype(F32)
            buffer[span, :] = sums.astype(BF16)
            copies.append(
                pltpu.make_async_copy(
                    buffer.at[pl.ds(part * rows, rows)],
                    out.at[pl.ds(pl.multiple_of(frame * FRAME_TOK + part * rows, rows), rows)],
                    sems.at[part],
                )
            )
            copies[-1].start()
        for copy in copies:
            copy.wait()

    operands = [attended, out_weight, *(array for array, _, _ in flat)]
    in_specs = [VMEM] * len(operands)
    aliases = {}
    if into is not None:
        aliases = {len(operands): 0}
        operands.append(into)
        in_specs.append(HBM)
    return pl.pallas_call(
        kernel,
        out_shape=jax.ShapeDtypeStruct((frames_here * FRAME_TOK, width), BF16),
        in_specs=in_specs,
        out_specs=HBM,
        scratch_shapes=[pltpu.VMEM((FRAME_TOK, width), BF16), pltpu.SemaphoreType.DMA((parts,))],
        input_output_aliases=aliases,
        compiler_params=params(),
    )(*operands)


def body(query_tok, key_tok, value_tok, head_span, out_weight):
    frames = lax.axis_size("frame")
    groups = lax.axis_size("head")
    local_frames = key_tok.shape[0] // FRAME_TOK
    bits = groups.bit_length() - 1
    assert local_frames == 2 and frames % 2 == 0 and groups == 1 << bits and FRAME_TOK % bits == 0
    seat = lax.axis_index("frame")
    parity = seat % 2
    link = jnp.where(parity == 0, seat > 0, seat < frames - 1)
    far_link = jnp.where(parity == 0, seat < frames - 2, seat > 1)
    table = jnp.concatenate(
        [jnp.stack([parity, link, far_link]).astype(jnp.int32), head_span.astype(jnp.int32)]
    )

    def swap(value):
        return lax.ppermute(value, "frame", [(i, i ^ 1) for i in range(frames)])

    def across(value):
        pairs = [(i, i + 1) for i in range(1, frames - 1, 2)]
        return lax.ppermute(value, "frame", pairs + [(b, a) for a, b in pairs])

    edge, inner = pack_frames(key_tok, value_tok)
    near = across(edge)
    partner_inner = swap(inner)
    partner_edge = swap(edge)
    second = across(inner)
    third = across(partner_inner)
    state = attend_step(
        table,
        query_tok,
        [edge, inner, partner_inner, partner_edge],
        {
            "E": (None, [(0, 0, None), (1, 1, None), (2, 2, None), (3, 3, None)]),
            "I": (None, [(1, 0, None), (0, 1, None), (2, 1, None), (3, 2, None)]),
        },
        True,
        False,
    )
    beyond = swap(near)
    state = attend_step(
        table,
        query_tok,
        [near, beyond],
        {"E": (state["E"], [(0, 1, 1)]), "I": (state["I"], [(0, 2, 1), (1, 3, 2)])},
        False,
        False,
    )
    attended = {}
    attended["I"] = attend_step(
        table, query_tok, [second], {"I": (state["I"], [(0, 3, 1)])}, False, True
    )["I"][0]

    def exchange(value, bit):
        return lax.ppermute(value, "head", [(i, i ^ (1 << bit)) for i in range(groups)])

    held = {role: [list(range(groups)) for _ in range(bits)] for role in "IE"}
    received = {role: [[] for _ in range(bits)] for role in "IE"}

    def gathered(role, part, slots):
        return [(array, [kept.index(s) for s in slots]) for array, kept in received[role][part]]

    def halve(role, stage):
        for part in range(bits):
            bit = (part + stage) % bits
            sent = [s for s in held[role][part] if s >> bit & 1]
            kept = [s for s in held[role][part] if not s >> bit & 1]
            terms = project(
                attended[role], part, bits, out_weight, sent, gathered(role, part, sent)
            )
            received[role][part].append((exchange(terms, bit), kept))
            held[role][part] = kept

    halve("I", 0)
    attended["E"] = attend_step(
        table, query_tok, [second, third], {"E": (state["E"], [(0, 2, 1), (1, 3, 1)])}, False, True
    )["E"][0]
    for stage in range(bits):
        halve("E", stage)
        if stage + 1 < bits:
            halve("I", stage + 1)
    result = None
    for role in "IE":
        result = finish(
            attended[role],
            bits,
            out_weight,
            [gathered(role, part, [0]) for part in range(bits)],
            role == "E",
            local_frames,
            result,
        )
    return result


def solution(mesh):
    return jax.shard_map(
        body,
        mesh=mesh,
        in_specs=(
            P("frame", "head"),
            P("frame", "head"),
            P("frame", "head"),
            P("head"),
            P("head", None),
        ),
        out_specs=P("frame", "head"),
        check_vma=False,
    )
```

```python
import jax
import jax.numpy as jnp
from jax import lax
from jax.experimental import pallas as pl
from jax.experimental.pallas import tpu as pltpu
from jax.sharding import PartitionSpec as P


HD = 128
FRAME_TOK = 384
LOG2E = 1.4426950408889634
F32 = jnp.float32
BF16 = jnp.bfloat16
VMEM_LIMIT = 16 << 20
CHUNK = 384
PAIRS = True


def params():
    return pltpu.CompilerParams(vmem_limit_bytes=VMEM_LIMIT)


VMEM = pl.BlockSpec(memory_space=pltpu.VMEM)
SMEM = pl.BlockSpec(memory_space=pltpu.SMEM)
HBM = pl.BlockSpec(memory_space=pltpu.HBM)


def pack_frames(key_tok, value_tok):
    parity = lax.axis_index("frame") % 2

    def packed(frame):
        return jnp.concatenate(
            [
                lax.dynamic_slice_in_dim(array, frame * FRAME_TOK, FRAME_TOK, 0)
                for array in (key_tok, value_tok)
            ],
            axis=0,
        )

    return packed(parity), packed(1 - parity)


def attend_step(table, query_tok, sources, states, cases, first, last):
    heads = query_tok.shape[1] // HD
    names = list(states)
    scale = LOG2E / HD**0.5
    per_role = 1 if last else 3

    def kernel(table_ref, query, *refs):
        refs = list(refs)
        chosen = refs.pop()
        loaded = [refs.pop(0) for _ in sources]
        olds = {} if first else {role: [refs.pop(0) for _ in range(3)] for role in names}
        outs = {role: [refs.pop(0) for _ in range(per_role)] for role in names}
        parity, link, far_link = table_ref[0], table_ref[1] > 0, table_ref[2] > 0
        starts = {"E": parity * FRAME_TOK, "I": (1 - parity) * FRAME_TOK}

        def wide(tops, times):
            return jnp.concatenate([tops] * times, axis=1)

        def take(heads_now, items):
            work = []
            for head in heads_now:
                column = pl.ds(pl.multiple_of(head * HD, HD), HD)
                for role, picked in items:
                    keys = jnp.concatenate([loaded[i][:FRAME_TOK, column] for i in picked], axis=0)
                    values = jnp.concatenate([loaded[i][FRAME_TOK:, column] for i in picked], axis=0)
                    values = jnp.concatenate([values, jnp.ones_like(values)], axis=1)
                    for at in range(0, FRAME_TOK, CHUNK):
                        work.append((role, column, slice(at, at + CHUNK), keys, values, len(picked)))
            done = []
            for role, column, rows, keys, values, count in work:
                here = pl.ds(pl.multiple_of(starts[role] + rows.start, CHUNK), CHUNK)
                scores = lax.dot_general(
                    query[here, column], keys, (((1,), (1,)), ((), ())), preferred_element_type=F32
                )
                top = jnp.broadcast_to(jnp.max(scores, axis=1, keepdims=True), (CHUNK, HD))
                fade = None
                if not first:
                    old_top = olds[role][2][rows, column]
                    top = jnp.maximum(top, old_top)
                    fade = jnp.exp2((old_top - top) * scale)
                times = count * FRAME_TOK // HD
                weights = jnp.exp2((scores - wide(top, times)) * scale).astype(BF16)
                mixed = jnp.dot(weights, values, preferred_element_type=F32)
                done.append((role, column, rows, mixed, top, fade))
            for role, column, rows, mixed, top, fade in done:
                acc, total = mixed[:, :HD], mixed[:, HD:]
                if not first:
                    acc = olds[role][0][rows, column] * fade + acc
                    total = olds[role][1][rows, column] * fade + total
                if last:
                    outs[role][0][rows, column] = (acc / total).astype(BF16)
                else:
                    outs[role][0][rows, column] = acc
                    outs[role][1][rows, column] = total
                    outs[role][2][rows, column] = top

        def close(head):
            column = pl.ds(pl.multiple_of(head * HD, HD), HD)
            for role in names:
                outs[role][0][:, column] = (olds[role][0][:, column] / olds[role][1][:, column]).astype(BF16)

        def collect(condition):
            def add(head, count):
                chosen[count] = head
                return count + condition(table_ref[3 + head], link, far_link).astype(jnp.int32)

            return lax.fori_loop(0, heads, add, jnp.int32(0))

        for condition, items in cases:
            count = collect(condition)
            if items:
                if PAIRS:

                    def pair(step, carry, items=items):
                        take((chosen[2 * step], chosen[2 * step + 1]), items)
                        return carry

                    lax.fori_loop(0, count // 2, pair, 0)
                    pl.when(count % 2 == 1)(lambda items=items: take((chosen[count - 1],), items))
                else:

                    def single(step, carry, items=items):
                        take((chosen[step],), items)
                        return carry

                    lax.fori_loop(0, count, single, 0)
            else:

                def plain(step, carry):
                    close(chosen[step])
                    return carry

                lax.fori_loop(0, count, plain, 0)

    operands = [table, query_tok, *sources]
    aliases = {}
    if not first:
        for index, role in enumerate(names):
            if not last:
                aliases.update({len(operands) + i: 3 * index + i for i in range(3)})
            operands += list(states[role])
    shape = jax.ShapeDtypeStruct((FRAME_TOK, heads * HD), BF16 if last else F32)
    count = per_role * len(names)
    out = pl.pallas_call(
        kernel,
        out_shape=(shape,) * count,
        in_specs=[SMEM] + [VMEM] * (len(operands) - 1),
        out_specs=(VMEM,) * count,
        scratch_shapes=[pltpu.SMEM((heads + 1,), jnp.int32)],
        input_output_aliases=aliases,
        compiler_params=params(),
    )(*operands)
    return {role: out[i * per_role : (i + 1) * per_role] for i, role in enumerate(names)}


def attend_chip(table, query_tok, edge, inner, partner_inner, partner_edge):
    order = {"E": [0, 1, 2, 3], "I": [1, 0, 2, 3]}
    reach = {"E": [1, 2, 3, 4], "I": [1, 3, 4, 4]}
    cases = [
        (
            lambda span, link, far_link, limit=limit: span == limit,
            [(role, order[role][: reach[role][limit]]) for role in "EI"],
        )
        for limit in range(4)
    ]
    return attend_step(
        table, query_tok, [edge, inner, partner_inner, partner_edge], {"E": None, "I": None}, cases, True, False
    )


def attend_near(table, query_tok, state, near, beyond):
    cases = [
        (lambda span, link, far_link: (span >= 3) & link & far_link, [("E", [0]), ("I", [0, 1])]),
        (
            lambda span, link, far_link: link & ((span == 2) | ((span >= 3) & jnp.logical_not(far_link))),
            [("E", [0]), ("I", [0])],
        ),
        (lambda span, link, far_link: (span == 1) & link, [("E", [0])]),
        (lambda span, link, far_link: (span >= 3) & jnp.logical_not(link) & far_link, [("I", [1])]),
    ]
    return attend_step(table, query_tok, [near, beyond], state, cases, False, False)


def attend_inner(table, query_tok, state, second):
    cases = [
        (lambda span, link, far_link: (span >= 3) & link, [("I", [0])]),
        (lambda span, link, far_link: (span < 3) | jnp.logical_not(link), []),
    ]
    return attend_step(table, query_tok, [second], state, cases, False, True)["I"][0]


def attend_edge(table, query_tok, state, second, third):
    cases = [
        (lambda span, link, far_link: (span >= 3) & link, [("E", [0, 1])]),
        (lambda span, link, far_link: (span == 2) & link, [("E", [0])]),
        (lambda span, link, far_link: (span < 2) | jnp.logical_not(link), []),
    ]
    return attend_step(table, query_tok, [second, third], state, cases, False, True)["E"][0]


def project(attended, part, parts, out_weight, slots, received):
    groups = lax.axis_size("head")
    width = out_weight.shape[1] // groups
    rows = attended.shape[0] // parts

    def kernel(left, right, *rest):
        out = rest[-1]
        group = lax.axis_index("head")
        for index, slot in enumerate(slots):
            column = pl.ds(pl.multiple_of((group ^ slot) * width, width), width)
            sums = jnp.dot(
                left[part * rows : (part + 1) * rows, :], right[:, column], preferred_element_type=F32
            )
            for ref, (_, spots) in zip(rest, received):
                sums = sums + ref[:, spots[index] * width : (spots[index] + 1) * width].astype(F32)
            out[:, index * width : (index + 1) * width] = sums.astype(BF16)

    return pl.pallas_call(
        kernel,
        out_shape=jax.ShapeDtypeStruct((rows, len(slots) * width), BF16),
        in_specs=[VMEM] * (2 + len(received)),
        out_specs=VMEM,
        compiler_params=params(),
    )(attended, out_weight, *(array for array, _ in received))


def finish(attended, parts, out_weight, received, is_edge, frames_here, into):
    groups = lax.axis_size("head")
    width = out_weight.shape[1] // groups
    rows = FRAME_TOK // parts
    flat = [(array, spots[0], part) for part in range(parts) for array, spots in received[part]]

    def kernel(left, right, *rest):
        out, buffer, sems = rest[-3:]
        group = lax.axis_index("head")
        parity = lax.axis_index("frame") % 2
        frame = parity if is_edge else 1 - parity
        column = pl.ds(pl.multiple_of(group * width, width), width)
        copies = []
        for part in range(parts):
            span = slice(part * rows, (part + 1) * rows)
            sums = jnp.dot(left[span, :], right[:, column], preferred_element_type=F32)
            for ref, (_, spot, owner) in zip(rest, flat):
                if owner == part:
                    sums = sums + ref[:, spot * width : (spot + 1) * width].astype(F32)
            buffer[span, :] = sums.astype(BF16)
            copies.append(
                pltpu.make_async_copy(
                    buffer.at[pl.ds(part * rows, rows)],
                    out.at[pl.ds(pl.multiple_of(frame * FRAME_TOK + part * rows, rows), rows)],
                    sems.at[part],
                )
            )
            copies[-1].start()
        for copy in copies:
            copy.wait()

    operands = [attended, out_weight, *(array for array, _, _ in flat)]
    in_specs = [VMEM] * len(operands)
    aliases = {}
    if into is not None:
        aliases = {len(operands): 0}
        operands.append(into)
        in_specs.append(HBM)
    return pl.pallas_call(
        kernel,
        out_shape=jax.ShapeDtypeStruct((frames_here * FRAME_TOK, width), BF16),
        in_specs=in_specs,
        out_specs=HBM,
        scratch_shapes=[pltpu.VMEM((FRAME_TOK, width), BF16), pltpu.SemaphoreType.DMA((parts,))],
        input_output_aliases=aliases,
        compiler_params=params(),
    )(*operands)


def body(query_tok, key_tok, value_tok, head_span, out_weight):
    frames = lax.axis_size("frame")
    groups = lax.axis_size("head")
    local_frames = key_tok.shape[0] // FRAME_TOK
    bits = groups.bit_length() - 1
    assert local_frames == 2 and frames % 2 == 0 and groups == 1 << bits and FRAME_TOK % bits == 0
    seat = lax.axis_index("frame")
    parity = seat % 2
    link = jnp.where(parity == 0, seat > 0, seat < frames - 1)
    far_link = jnp.where(parity == 0, seat < frames - 2, seat > 1)
    table = jnp.concatenate(
        [jnp.stack([parity, link, far_link]).astype(jnp.int32), head_span.astype(jnp.int32)]
    )

    def swap(value):
        return lax.ppermute(value, "frame", [(i, i ^ 1) for i in range(frames)])

    def across(value):
        pairs = [(i, i + 1) for i in range(1, frames - 1, 2)]
        return lax.ppermute(value, "frame", pairs + [(b, a) for a, b in pairs])

    edge, inner = pack_frames(key_tok, value_tok)
    near = across(edge)
    partner_inner = swap(inner)
    partner_edge = swap(edge)
    second = across(inner)
    third = across(partner_inner)
    state = attend_chip(table, query_tok, edge, inner, partner_inner, partner_edge)
    beyond = swap(near)
    state = attend_near(table, query_tok, state, near, beyond)
    attended = {"I": attend_inner(table, query_tok, {"I": state["I"]}, second)}

    def exchange(value, bit):
        return lax.ppermute(value, "head", [(i, i ^ (1 << bit)) for i in range(groups)])

    held = {role: [list(range(groups)) for _ in range(bits)] for role in "IE"}
    received = {role: [[] for _ in range(bits)] for role in "IE"}

    def gathered(role, part, slots):
        return [(array, [kept.index(s) for s in slots]) for array, kept in received[role][part]]

    def halve(role, stage):
        for part in range(bits):
            bit = (part + stage) % bits
            sent = [s for s in held[role][part] if s >> bit & 1]
            kept = [s for s in held[role][part] if not s >> bit & 1]
            terms = project(attended[role], part, bits, out_weight, sent, gathered(role, part, sent))
            received[role][part].append((exchange(terms, bit), kept))
            held[role][part] = kept

    halve("I", 0)
    attended["E"] = attend_edge(table, query_tok, {"E": state["E"]}, second, third)
    for stage in range(bits):
        halve("E", stage)
        if stage + 1 < bits:
            halve("I", stage + 1)
    result = None
    for role in "IE":
        result = finish(
            attended[role],
            bits,
            out_weight,
            [gathered(role, part, [0]) for part in range(bits)],
            role == "E",
            local_frames,
            result,
        )
    return result


def solution(mesh):
    return jax.shard_map(
        body,
        mesh=mesh,
        in_specs=(
            P("frame", "head"),
            P("frame", "head"),
            P("frame", "head"),
            P("head"),
            P("head", None),
        ),
        out_specs=P("frame", "head"),
        check_vma=False,
    )
```

```python
import jax
import jax.numpy as jnp
from jax import lax
from jax.experimental import pallas as pl
from jax.experimental.pallas import tpu as pltpu
from jax.sharding import PartitionSpec as P


HD = 128
FRAME_TOK = 384
LOG2E = 1.4426950408889634
F32 = jnp.float32
BF16 = jnp.bfloat16
VMEM_LIMIT = 16 << 20
CHUNK = 384


def params():
    return pltpu.CompilerParams(vmem_limit_bytes=VMEM_LIMIT)


VMEM = pl.BlockSpec(memory_space=pltpu.VMEM)
SMEM = pl.BlockSpec(memory_space=pltpu.SMEM)
HBM = pl.BlockSpec(memory_space=pltpu.HBM)


def pack_frames(key_tok, value_tok):
    parity = lax.axis_index("frame") % 2

    def packed(frame):
        return jnp.concatenate(
            [
                lax.dynamic_slice_in_dim(array, frame * FRAME_TOK, FRAME_TOK, 0)
                for array in (key_tok, value_tok)
            ],
            axis=0,
        )

    return packed(parity), packed(1 - parity)


def attend_step(table, query_tok, sources, states, cases, first=False, closed=None):
    heads = query_tok.shape[1] // HD
    names = list(states)
    closed = closed or {}
    scale = LOG2E / HD**0.5
    keep = first or any(items and not close for _, items, close in cases)

    def kernel(table_ref, query, *refs):
        refs = list(refs)
        chosen = refs.pop()
        loaded = [refs.pop(0) for _ in sources]
        olds = {} if first else {role: [refs.pop(0) for _ in range(3)] for role in names}
        for role in closed:
            if closed[role] is not None:
                refs.pop(0)
        outs = {role: [refs.pop(0) for _ in range(3)] for role in names} if keep else {}
        results = {role: refs.pop(0) for role in closed}
        reads = outs if keep and not first else olds
        parity, link, far_link = table_ref[0], table_ref[1] > 0, table_ref[2] > 0
        starts = {"E": parity * FRAME_TOK, "I": (1 - parity) * FRAME_TOK}

        def wide(tops, times):
            return jnp.concatenate([tops] * times, axis=1)

        def take(heads_now, items, close):
            work = []
            for head in heads_now:
                column = pl.ds(pl.multiple_of(head * HD, HD), HD)
                for role, picked in items:
                    keys = jnp.concatenate([loaded[i][:FRAME_TOK, column] for i in picked], axis=0)
                    values = jnp.concatenate([loaded[i][FRAME_TOK:, column] for i in picked], axis=0)
                    values = jnp.concatenate([values, jnp.ones_like(values)], axis=1)
                    for at in range(0, FRAME_TOK, CHUNK):
                        work.append((role, column, slice(at, at + CHUNK), keys, values, len(picked)))
            done = []
            for role, column, rows, keys, values, count in work:
                here = pl.ds(pl.multiple_of(starts[role] + rows.start, CHUNK), CHUNK)
                scores = lax.dot_general(
                    query[here, column], keys, (((1,), (1,)), ((), ())), preferred_element_type=F32
                )
                top = jnp.broadcast_to(jnp.max(scores, axis=1, keepdims=True), (CHUNK, HD))
                fade = None
                if not first:
                    old_top = reads[role][2][rows, column]
                    top = jnp.maximum(top, old_top)
                    fade = jnp.exp2((old_top - top) * scale)
                times = count * FRAME_TOK // HD
                weights = jnp.exp2((scores - wide(top, times)) * scale).astype(BF16)
                mixed = jnp.dot(weights, values, preferred_element_type=F32)
                done.append((role, column, rows, mixed, top, fade))
            for role, column, rows, mixed, top, fade in done:
                acc, total = mixed[:, :HD], mixed[:, HD:]
                if not first:
                    acc = reads[role][0][rows, column] * fade + acc
                    total = reads[role][1][rows, column] * fade + total
                if role in close:
                    results[role][rows, column] = (acc / total).astype(BF16)
                else:
                    outs[role][0][rows, column] = acc
                    outs[role][1][rows, column] = total
                    outs[role][2][rows, column] = top

        def finish_head(head, roles):
            column = pl.ds(pl.multiple_of(head * HD, HD), HD)
            for role in roles:
                acc, total = reads[role][0][:, column], reads[role][1][:, column]
                results[role][:, column] = (acc / total).astype(BF16)

        def collect(condition):
            def add(head, count):
                chosen[count] = head
                return count + condition(table_ref[3 + head], link, far_link).astype(jnp.int32)

            return lax.fori_loop(0, heads, add, jnp.int32(0))

        for condition, items, close in cases:
            count = collect(condition)
            if items:

                def pair(step, carry, items=items, close=close):
                    take((chosen[2 * step], chosen[2 * step + 1]), items, close)
                    return carry

                lax.fori_loop(0, count // 2, pair, 0)
                pl.when(count % 2 == 1)(
                    lambda items=items, close=close, count=count: take((chosen[count - 1],), items, close)
                )
            else:

                def plain(step, carry, close=close):
                    finish_head(chosen[step], close)
                    return carry

                lax.fori_loop(0, count, plain, 0)

    operands = [table, query_tok, *sources]
    shapes = []
    aliases = {}
    if not first:
        for index, role in enumerate(names):
            if keep:
                aliases.update({len(operands) + i: 3 * index + i for i in range(3)})
            operands += list(states[role])
    if keep:
        shapes += [jax.ShapeDtypeStruct((FRAME_TOK, heads * HD), F32)] * (3 * len(names))
    for role in closed:
        if closed[role] is not None:
            aliases[len(operands)] = len(shapes)
            operands.append(closed[role])
        shapes.append(jax.ShapeDtypeStruct((FRAME_TOK, heads * HD), BF16))
    out = list(
        pl.pallas_call(
            kernel,
            out_shape=tuple(shapes),
            in_specs=[SMEM] + [VMEM] * (len(operands) - 1),
            out_specs=(VMEM,) * len(shapes),
            scratch_shapes=[pltpu.SMEM((heads + 1,), jnp.int32)],
            input_output_aliases=aliases,
            compiler_params=params(),
        )(*operands)
    )
    new_states = {role: [out.pop(0) for _ in range(3)] for role in names} if keep else {}
    return new_states, {role: out.pop(0) for role in closed}


def attend_chip(table, query_tok, edge, inner, partner_inner, partner_edge):
    order = {"E": [0, 1, 2, 3], "I": [1, 0, 2, 3]}
    reach = {"E": [1, 2, 3, 4], "I": [1, 3, 4, 4]}
    cases = [
        (
            lambda span, link, far_link, limit=limit: span == limit,
            [(role, order[role][: reach[role][limit]]) for role in "EI"],
            "",
        )
        for limit in range(4)
    ]
    return attend_step(
        table, query_tok, [edge, inner, partner_inner, partner_edge], {"E": None, "I": None}, cases, first=True
    )[0]


def attend_near(table, query_tok, state, near):
    cases = [
        (lambda span, link, far_link: (span >= 2) & link, [("E", [0]), ("I", [0])], ""),
        (lambda span, link, far_link: (span == 1) & link, [("E", [0])], ""),
    ]
    return attend_step(table, query_tok, [near], state, cases)[0]


def attend_beyond(table, query_tok, state, beyond):
    cases = [
        (lambda span, link, far_link: (span >= 3) & far_link, [("I", [0])], ""),
        (lambda span, link, far_link: (span < 3) | jnp.logical_not(link), [], "I"),
        (lambda span, link, far_link: (span < 2) | jnp.logical_not(link), [], "E"),
    ]
    return attend_step(table, query_tok, [beyond], state, cases, closed={"I": None, "E": None})


def attend_inner(table, query_tok, state, second, result):
    cases = [(lambda span, link, far_link: (span >= 3) & link, [("I", [0])], "I")]
    return attend_step(table, query_tok, [second], {"I": state}, cases, closed={"I": result})[1]["I"]


def attend_edge(table, query_tok, state, second, third, result):
    cases = [
        (lambda span, link, far_link: (span >= 3) & link, [("E", [0, 1])], "E"),
        (lambda span, link, far_link: (span == 2) & link, [("E", [0])], "E"),
    ]
    return attend_step(table, query_tok, [second, third], {"E": state}, cases, closed={"E": result})[1]["E"]


def project(attended, part, parts, out_weight, slots, received):
    groups = lax.axis_size("head")
    width = out_weight.shape[1] // groups
    rows = attended.shape[0] // parts

    def kernel(left, right, *rest):
        out = rest[-1]
        group = lax.axis_index("head")
        for index, slot in enumerate(slots):
            column = pl.ds(pl.multiple_of((group ^ slot) * width, width), width)
            sums = jnp.dot(
                left[part * rows : (part + 1) * rows, :], right[:, column], preferred_element_type=F32
            )
            for ref, (_, spots) in zip(rest, received):
                sums = sums + ref[:, spots[index] * width : (spots[index] + 1) * width].astype(F32)
            out[:, index * width : (index + 1) * width] = sums.astype(BF16)

    return pl.pallas_call(
        kernel,
        out_shape=jax.ShapeDtypeStruct((rows, len(slots) * width), BF16),
        in_specs=[VMEM] * (2 + len(received)),
        out_specs=VMEM,
        compiler_params=params(),
    )(attended, out_weight, *(array for array, _ in received))


def finish(attended, parts, out_weight, received, is_edge, frames_here, into):
    groups = lax.axis_size("head")
    width = out_weight.shape[1] // groups
    rows = FRAME_TOK // parts
    flat = [(array, spots[0], part) for part in range(parts) for array, spots in received[part]]

    def kernel(left, right, *rest):
        out, buffer, sems = rest[-3:]
        group = lax.axis_index("head")
        parity = lax.axis_index("frame") % 2
        frame = parity if is_edge else 1 - parity
        column = pl.ds(pl.multiple_of(group * width, width), width)
        copies = []
        for part in range(parts):
            span = slice(part * rows, (part + 1) * rows)
            sums = jnp.dot(left[span, :], right[:, column], preferred_element_type=F32)
            for ref, (_, spot, owner) in zip(rest, flat):
                if owner == part:
                    sums = sums + ref[:, spot * width : (spot + 1) * width].astype(F32)
            buffer[span, :] = sums.astype(BF16)
            copies.append(
                pltpu.make_async_copy(
                    buffer.at[pl.ds(part * rows, rows)],
                    out.at[pl.ds(pl.multiple_of(frame * FRAME_TOK + part * rows, rows), rows)],
                    sems.at[part],
                )
            )
            copies[-1].start()
        for copy in copies:
            copy.wait()

    operands = [attended, out_weight, *(array for array, _, _ in flat)]
    in_specs = [VMEM] * len(operands)
    aliases = {}
    if into is not None:
        aliases = {len(operands): 0}
        operands.append(into)
        in_specs.append(HBM)
    return pl.pallas_call(
        kernel,
        out_shape=jax.ShapeDtypeStruct((frames_here * FRAME_TOK, width), BF16),
        in_specs=in_specs,
        out_specs=HBM,
        scratch_shapes=[pltpu.VMEM((FRAME_TOK, width), BF16), pltpu.SemaphoreType.DMA((parts,))],
        input_output_aliases=aliases,
        compiler_params=params(),
    )(*operands)


def body(query_tok, key_tok, value_tok, head_span, out_weight):
    frames = lax.axis_size("frame")
    groups = lax.axis_size("head")
    local_frames = key_tok.shape[0] // FRAME_TOK
    bits = groups.bit_length() - 1
    assert local_frames == 2 and frames % 2 == 0 and groups == 1 << bits and FRAME_TOK % bits == 0
    seat = lax.axis_index("frame")
    parity = seat % 2
    link = jnp.where(parity == 0, seat > 0, seat < frames - 1)
    far_link = jnp.where(parity == 0, seat < frames - 2, seat > 1)
    table = jnp.concatenate(
        [jnp.stack([parity, link, far_link]).astype(jnp.int32), head_span.astype(jnp.int32)]
    )

    def swap(value):
        return lax.ppermute(value, "frame", [(i, i ^ 1) for i in range(frames)])

    def across(value):
        pairs = [(i, i + 1) for i in range(1, frames - 1, 2)]
        return lax.ppermute(value, "frame", pairs + [(b, a) for a, b in pairs])

    edge, inner = pack_frames(key_tok, value_tok)
    near = across(edge)
    partner_inner = swap(inner)
    partner_edge = swap(edge)
    second = across(inner)
    third = across(partner_inner)
    state = attend_chip(table, query_tok, edge, inner, partner_inner, partner_edge)
    beyond = swap(near)
    state = attend_near(table, query_tok, state, near)
    state, attended = attend_beyond(table, query_tok, state, beyond)
    attended["I"] = attend_inner(table, query_tok, state["I"], second, attended["I"])

    def exchange(value, bit):
        return lax.ppermute(value, "head", [(i, i ^ (1 << bit)) for i in range(groups)])

    held = {role: [list(range(groups)) for _ in range(bits)] for role in "IE"}
    received = {role: [[] for _ in range(bits)] for role in "IE"}

    def gathered(role, part, slots):
        return [(array, [kept.index(s) for s in slots]) for array, kept in received[role][part]]

    def halve(role, stage):
        for part in range(bits):
            bit = (part + stage) % bits
            sent = [s for s in held[role][part] if s >> bit & 1]
            kept = [s for s in held[role][part] if not s >> bit & 1]
            terms = project(attended[role], part, bits, out_weight, sent, gathered(role, part, sent))
            received[role][part].append((exchange(terms, bit), kept))
            held[role][part] = kept

    halve("I", 0)
    attended["E"] = attend_edge(table, query_tok, state["E"], second, third, attended["E"])
    for stage in range(bits):
        halve("E", stage)
        if stage + 1 < bits:
            halve("I", stage + 1)
    result = None
    for role in "IE":
        result = finish(
            attended[role],
            bits,
            out_weight,
            [gathered(role, part, [0]) for part in range(bits)],
            role == "E",
            local_frames,
            result,
        )
    return result


def solution(mesh):
    return jax.shard_map(
        body,
        mesh=mesh,
        in_specs=(
            P("frame", "head"),
            P("frame", "head"),
            P("frame", "head"),
            P("head"),
            P("head", None),
        ),
        out_specs=P("frame", "head"),
        check_vma=False,
    )
```

```python
import jax
import jax.numpy as jnp
from jax import lax
from jax.experimental import pallas as pl
from jax.experimental.pallas import tpu as pltpu
from jax.sharding import PartitionSpec as P


HD = 128
FRAME_TOK = 384
LOG2E = 1.4426950408889634
F32 = jnp.float32
BF16 = jnp.bfloat16
VMEM_LIMIT = 16 << 20
CHUNK = 384


def params():
    return pltpu.CompilerParams(vmem_limit_bytes=VMEM_LIMIT)


VMEM = pl.BlockSpec(memory_space=pltpu.VMEM)
SMEM = pl.BlockSpec(memory_space=pltpu.SMEM)
HBM = pl.BlockSpec(memory_space=pltpu.HBM)


def pack_frames(key_tok, value_tok):
    parity = lax.axis_index("frame") % 2

    def packed(key, value, frame):
        return jnp.concatenate(
            [lax.dynamic_slice_in_dim(array, frame * FRAME_TOK, FRAME_TOK, 0) for array in (key, value)],
            axis=0,
        )

    edge = packed(key_tok, value_tok, parity)
    edge, key_tok, value_tok = lax.optimization_barrier((edge, key_tok, value_tok))
    return edge, packed(key_tok, value_tok, 1 - parity)


def attend_step(table, query_tok, sources, states, cases, first=False, closed=None):
    heads = query_tok.shape[1] // HD
    names = list(states)
    closed = closed or {}
    scale = LOG2E / HD**0.5
    keep = first or any(items and not close for _, items, close in cases)

    def kernel(table_ref, query, *refs):
        refs = list(refs)
        chosen = refs.pop()
        loaded = [refs.pop(0) for _ in sources]
        olds = {} if first else {role: [refs.pop(0) for _ in range(3)] for role in names}
        for role in closed:
            if closed[role] is not None:
                refs.pop(0)
        outs = {role: [refs.pop(0) for _ in range(3)] for role in names} if keep else {}
        results = {role: refs.pop(0) for role in closed}
        reads = outs if keep and not first else olds
        parity, link, far_link = table_ref[0], table_ref[1] > 0, table_ref[2] > 0
        starts = {"E": parity * FRAME_TOK, "I": (1 - parity) * FRAME_TOK}

        def wide(tops, times):
            return jnp.concatenate([tops] * times, axis=1)

        def take(heads_now, items, close):
            work = []
            for head in heads_now:
                column = pl.ds(pl.multiple_of(head * HD, HD), HD)
                for role, picked in items:
                    keys = jnp.concatenate([loaded[i][:FRAME_TOK, column] for i in picked], axis=0)
                    values = jnp.concatenate([loaded[i][FRAME_TOK:, column] for i in picked], axis=0)
                    values = jnp.concatenate([values, jnp.ones_like(values)], axis=1)
                    for at in range(0, FRAME_TOK, CHUNK):
                        work.append((role, column, slice(at, at + CHUNK), keys, values, len(picked)))
            done = []
            for role, column, rows, keys, values, count in work:
                here = pl.ds(pl.multiple_of(starts[role] + rows.start, CHUNK), CHUNK)
                scores = lax.dot_general(
                    query[here, column], keys, (((1,), (1,)), ((), ())), preferred_element_type=F32
                )
                top = jnp.broadcast_to(jnp.max(scores, axis=1, keepdims=True), (CHUNK, HD))
                fade = None
                if not first:
                    old_top = reads[role][2][rows, column]
                    top = jnp.maximum(top, old_top)
                    fade = jnp.exp2((old_top - top) * scale)
                times = count * FRAME_TOK // HD
                weights = jnp.exp2((scores - wide(top, times)) * scale).astype(BF16)
                mixed = jnp.dot(weights, values, preferred_element_type=F32)
                done.append((role, column, rows, mixed, top, fade))
            for role, column, rows, mixed, top, fade in done:
                acc, total = mixed[:, :HD], mixed[:, HD:]
                if not first:
                    acc = reads[role][0][rows, column] * fade + acc
                    total = reads[role][1][rows, column] * fade + total
                if role in close:
                    results[role][rows, column] = (acc / total).astype(BF16)
                else:
                    outs[role][0][rows, column] = acc
                    outs[role][1][rows, column] = total
                    outs[role][2][rows, column] = top

        def finish_head(head, roles):
            column = pl.ds(pl.multiple_of(head * HD, HD), HD)
            for role in roles:
                acc, total = reads[role][0][:, column], reads[role][1][:, column]
                results[role][:, column] = (acc / total).astype(BF16)

        def collect(condition):
            def add(head, count):
                chosen[count] = head
                return count + condition(table_ref[3 + head], link, far_link).astype(jnp.int32)

            return lax.fori_loop(0, heads, add, jnp.int32(0))

        for condition, items, close in cases:
            count = collect(condition)
            if items:

                def pair(step, carry, items=items, close=close):
                    take((chosen[2 * step], chosen[2 * step + 1]), items, close)
                    return carry

                lax.fori_loop(0, count // 2, pair, 0)
                pl.when(count % 2 == 1)(
                    lambda items=items, close=close, count=count: take((chosen[count - 1],), items, close)
                )
            else:

                def plain(step, carry, close=close):
                    finish_head(chosen[step], close)
                    return carry

                lax.fori_loop(0, count, plain, 0)

    operands = [table, query_tok, *sources]
    shapes = []
    aliases = {}
    if not first:
        for index, role in enumerate(names):
            if keep:
                aliases.update({len(operands) + i: 3 * index + i for i in range(3)})
            operands += list(states[role])
    if keep:
        shapes += [jax.ShapeDtypeStruct((FRAME_TOK, heads * HD), F32)] * (3 * len(names))
    for role in closed:
        if closed[role] is not None:
            aliases[len(operands)] = len(shapes)
            operands.append(closed[role])
        shapes.append(jax.ShapeDtypeStruct((FRAME_TOK, heads * HD), BF16))
    out = list(
        pl.pallas_call(
            kernel,
            out_shape=tuple(shapes),
            in_specs=[SMEM] + [VMEM] * (len(operands) - 1),
            out_specs=(VMEM,) * len(shapes),
            scratch_shapes=[pltpu.SMEM((heads + 1,), jnp.int32)],
            input_output_aliases=aliases,
            compiler_params=params(),
        )(*operands)
    )
    new_states = {role: [out.pop(0) for _ in range(3)] for role in names} if keep else {}
    return new_states, {role: out.pop(0) for role in closed}


def attend_chip(table, query_tok, edge, inner, partner_inner, partner_edge):
    order = {"E": [0, 1, 2, 3], "I": [1, 0, 2, 3]}
    reach = {"E": [1, 2, 3, 4], "I": [1, 3, 4, 4]}
    cases = [
        (
            lambda span, link, far_link, limit=limit: span == limit,
            [(role, order[role][: reach[role][limit]]) for role in "EI"],
            "",
        )
        for limit in range(4)
    ]
    return attend_step(
        table, query_tok, [edge, inner, partner_inner, partner_edge], {"E": None, "I": None}, cases, first=True
    )[0]


def attend_near(table, query_tok, state, near):
    cases = [
        (lambda span, link, far_link: (span >= 2) & link, [("E", [0]), ("I", [0])], ""),
        (lambda span, link, far_link: (span == 1) & link, [("E", [0])], ""),
    ]
    return attend_step(table, query_tok, [near], state, cases)[0]


def attend_beyond(table, query_tok, state, beyond):
    cases = [
        (lambda span, link, far_link: (span >= 3) & far_link, [("I", [0])], ""),
        (lambda span, link, far_link: (span < 3) | jnp.logical_not(link), [], "I"),
        (lambda span, link, far_link: (span < 2) | jnp.logical_not(link), [], "E"),
    ]
    return attend_step(table, query_tok, [beyond], state, cases, closed={"I": None, "E": None})


def attend_inner(table, query_tok, state, second, result):
    cases = [(lambda span, link, far_link: (span >= 3) & link, [("I", [0])], "I")]
    return attend_step(table, query_tok, [second], {"I": state}, cases, closed={"I": result})[1]["I"]


def attend_edge(table, query_tok, state, second, third, result):
    cases = [
        (lambda span, link, far_link: (span >= 3) & link, [("E", [0, 1])], "E"),
        (lambda span, link, far_link: (span == 2) & link, [("E", [0])], "E"),
    ]
    return attend_step(table, query_tok, [second, third], {"E": state}, cases, closed={"E": result})[1]["E"]


def project(attended, part, parts, out_weight, slots, received):
    groups = lax.axis_size("head")
    width = out_weight.shape[1] // groups
    rows = attended.shape[0] // parts

    def kernel(left, right, *rest):
        out = rest[-1]
        group = lax.axis_index("head")
        for index, slot in enumerate(slots):
            column = pl.ds(pl.multiple_of((group ^ slot) * width, width), width)
            sums = jnp.dot(
                left[part * rows : (part + 1) * rows, :], right[:, column], preferred_element_type=F32
            )
            for ref, (_, spots) in zip(rest, received):
                sums = sums + ref[:, spots[index] * width : (spots[index] + 1) * width].astype(F32)
            out[:, index * width : (index + 1) * width] = sums.astype(BF16)

    return pl.pallas_call(
        kernel,
        out_shape=jax.ShapeDtypeStruct((rows, len(slots) * width), BF16),
        in_specs=[VMEM] * (2 + len(received)),
        out_specs=VMEM,
        compiler_params=params(),
    )(attended, out_weight, *(array for array, _ in received))


def sum_own(attended, parts, out_weight, received):
    groups = lax.axis_size("head")
    width = out_weight.shape[1] // groups
    rows = FRAME_TOK // parts
    flat = [(array, spots[0], part) for part in range(parts) for array, spots in received[part]]

    def kernel(left, right, *rest):
        out = rest[-1]
        group = lax.axis_index("head")
        column = pl.ds(pl.multiple_of(group * width, width), width)
        sums = jnp.dot(left[...], right[:, column], preferred_element_type=F32)
        for part in range(parts):
            terms = sums[part * rows : (part + 1) * rows]
            for ref, (_, spot, owner) in zip(rest, flat):
                if owner == part:
                    terms = terms + ref[:, spot * width : (spot + 1) * width].astype(F32)
            out[part * rows : (part + 1) * rows, :] = terms

    operands = [attended, out_weight, *(array for array, _, _ in flat)]
    return pl.pallas_call(
        kernel,
        out_shape=jax.ShapeDtypeStruct((FRAME_TOK, width), F32),
        in_specs=[VMEM] * len(operands),
        out_specs=VMEM,
        compiler_params=params(),
    )(*operands)


def finish(own, received, is_edge, frames_here, into):
    parts = len(received)
    rows = FRAME_TOK // parts
    width = own.shape[1]

    def kernel(terms, *rest):
        out, buffer, sems = rest[-3:]
        parity = lax.axis_index("frame") % 2
        frame = parity if is_edge else 1 - parity
        copies = []
        for part in range(parts):
            span = slice(part * rows, (part + 1) * rows)
            buffer[span, :] = (terms[span, :] + rest[part][...].astype(F32)).astype(BF16)
            copies.append(
                pltpu.make_async_copy(
                    buffer.at[pl.ds(part * rows, rows)],
                    out.at[pl.ds(pl.multiple_of(frame * FRAME_TOK + part * rows, rows), rows)],
                    sems.at[part],
                )
            )
            copies[-1].start()
        for copy in copies:
            copy.wait()

    operands = [own, *received]
    in_specs = [VMEM] * len(operands)
    aliases = {}
    if into is not None:
        aliases = {len(operands): 0}
        operands.append(into)
        in_specs.append(HBM)
    return pl.pallas_call(
        kernel,
        out_shape=jax.ShapeDtypeStruct((frames_here * FRAME_TOK, width), BF16),
        in_specs=in_specs,
        out_specs=HBM,
        scratch_shapes=[pltpu.VMEM((FRAME_TOK, width), BF16), pltpu.SemaphoreType.DMA((parts,))],
        input_output_aliases=aliases,
        compiler_params=params(),
    )(*operands)


def body(query_tok, key_tok, value_tok, head_span, out_weight):
    frames = lax.axis_size("frame")
    groups = lax.axis_size("head")
    local_frames = key_tok.shape[0] // FRAME_TOK
    bits = groups.bit_length() - 1
    assert local_frames == 2 and frames % 2 == 0 and groups == 1 << bits and FRAME_TOK % bits == 0
    seat = lax.axis_index("frame")
    parity = seat % 2
    link = jnp.where(parity == 0, seat > 0, seat < frames - 1)
    far_link = jnp.where(parity == 0, seat < frames - 2, seat > 1)
    table = jnp.concatenate(
        [jnp.stack([parity, link, far_link]).astype(jnp.int32), head_span.astype(jnp.int32)]
    )

    def swap(value):
        return lax.ppermute(value, "frame", [(i, i ^ 1) for i in range(frames)])

    def across(value):
        pairs = [(i, i + 1) for i in range(1, frames - 1, 2)]
        return lax.ppermute(value, "frame", pairs + [(b, a) for a, b in pairs])

    edge, inner = pack_frames(key_tok, value_tok)
    near = across(edge)
    partner_inner = swap(inner)
    partner_edge = swap(edge)
    second = across(inner)
    third = across(partner_inner)
    state = attend_chip(table, query_tok, edge, inner, partner_inner, partner_edge)
    beyond = swap(near)
    state = attend_near(table, query_tok, state, near)
    state, attended = attend_beyond(table, query_tok, state, beyond)
    attended["I"] = attend_inner(table, query_tok, state["I"], second, attended["I"])

    def exchange(value, bit):
        return lax.ppermute(value, "head", [(i, i ^ (1 << bit)) for i in range(groups)])

    held = {role: [list(range(groups)) for _ in range(bits)] for role in "IE"}
    received = {role: [[] for _ in range(bits)] for role in "IE"}

    def gathered(role, part, slots):
        return [(array, [kept.index(s) for s in slots]) for array, kept in received[role][part]]

    def halve(role, stage):
        for part in range(bits):
            bit = (part + stage) % bits
            sent = [s for s in held[role][part] if s >> bit & 1]
            kept = [s for s in held[role][part] if not s >> bit & 1]
            terms = project(attended[role], part, bits, out_weight, sent, gathered(role, part, sent))
            received[role][part].append((exchange(terms, bit), kept))
            held[role][part] = kept

    halve("I", 0)
    attended["E"] = attend_edge(table, query_tok, state["E"], second, third, attended["E"])
    for stage in range(bits):
        halve("E", stage)
        if stage + 1 < bits:
            halve("I", stage + 1)
    result = None
    for role in "IE":
        terms = [gathered(role, part, [0]) for part in range(bits)]
        own = sum_own(attended[role], bits, out_weight, [t[:-1] for t in terms])
        result = finish(own, [t[-1][0] for t in terms], role == "E", local_frames, result)
    return result


def solution(mesh):
    return jax.shard_map(
        body,
        mesh=mesh,
        in_specs=(
            P("frame", "head"),
            P("frame", "head"),
            P("frame", "head"),
            P("head"),
            P("head", None),
        ),
        out_specs=P("frame", "head"),
        check_vma=False,
    )
```

```python
import jax
import jax.numpy as jnp
from jax import lax
from jax.experimental import pallas as pl
from jax.experimental.pallas import tpu as pltpu
from jax.sharding import PartitionSpec as P


HD = 128
FRAME_TOK = 384
LOG2E = 1.4426950408889634
F32 = jnp.float32
BF16 = jnp.bfloat16
VMEM_LIMIT = 16 << 20
CHUNK = 384


def params():
    return pltpu.CompilerParams(vmem_limit_bytes=VMEM_LIMIT)


VMEM = pl.BlockSpec(memory_space=pltpu.VMEM)
SMEM = pl.BlockSpec(memory_space=pltpu.SMEM)
HBM = pl.BlockSpec(memory_space=pltpu.HBM)


def pack_frames(key_tok, value_tok):
    parity = lax.axis_index("frame") % 2

    def packed(key, value, frame):
        rows = [lax.dynamic_slice_in_dim(array, frame * FRAME_TOK, FRAME_TOK, 0) for array in (key, value)]
        return jnp.concatenate(rows, axis=0)

    edge = packed(key_tok, value_tok, parity)
    edge, key_tok, value_tok = lax.optimization_barrier((edge, key_tok, value_tok))
    return edge, packed(key_tok, value_tok, 1 - parity)


def attend_step(table, query_tok, sources, states, cases, first=False, closed=None):
    heads = query_tok.shape[1] // HD
    names = list(states)
    closed = closed or {}
    scale = LOG2E / HD**0.5
    keep = first or any(items and not close for _, items, close in cases)

    def kernel(table_ref, query, *refs):
        refs = list(refs)
        chosen = refs.pop()
        loaded = [refs.pop(0) for _ in sources]
        olds = {} if first else {role: [refs.pop(0) for _ in range(3)] for role in names}
        for role in closed:
            if closed[role] is not None:
                refs.pop(0)
        outs = {role: [refs.pop(0) for _ in range(3)] for role in names} if keep else {}
        results = {role: refs.pop(0) for role in closed}
        reads = outs if keep and not first else olds
        parity, link, far_link = table_ref[0], table_ref[1] > 0, table_ref[2] > 0
        starts = {"E": parity * FRAME_TOK, "I": (1 - parity) * FRAME_TOK}

        def wide(tops, times):
            return jnp.concatenate([tops] * times, axis=1)

        def take(heads_now, items, close):
            work = []
            for head in heads_now:
                column = pl.ds(pl.multiple_of(head * HD, HD), HD)
                for role, picked in items:
                    keys = jnp.concatenate([loaded[i][:FRAME_TOK, column] for i in picked], axis=0)
                    values = jnp.concatenate([loaded[i][FRAME_TOK:, column] for i in picked], axis=0)
                    values = jnp.concatenate([values, jnp.ones_like(values)], axis=1)
                    for at in range(0, FRAME_TOK, CHUNK):
                        work.append((role, column, slice(at, at + CHUNK), keys, values, len(picked)))
            done = []
            for role, column, rows, keys, values, count in work:
                here = pl.ds(pl.multiple_of(starts[role] + rows.start, CHUNK), CHUNK)
                scores = lax.dot_general(
                    query[here, column], keys, (((1,), (1,)), ((), ())), preferred_element_type=F32
                )
                top = jnp.broadcast_to(jnp.max(scores, axis=1, keepdims=True), (CHUNK, HD))
                fade = None
                if not first:
                    old_top = reads[role][2][rows, column]
                    top = jnp.maximum(top, old_top)
                    fade = jnp.exp2((old_top - top) * scale)
                times = count * FRAME_TOK // HD
                weights = jnp.exp2((scores - wide(top, times)) * scale).astype(BF16)
                mixed = jnp.dot(weights, values, preferred_element_type=F32)
                done.append((role, column, rows, mixed, top, fade))
            for role, column, rows, mixed, top, fade in done:
                acc, total = mixed[:, :HD], mixed[:, HD:]
                if not first:
                    acc = reads[role][0][rows, column] * fade + acc
                    total = reads[role][1][rows, column] * fade + total
                if role in close:
                    results[role][rows, column] = (acc / total).astype(BF16)
                else:
                    outs[role][0][rows, column] = acc
                    outs[role][1][rows, column] = total
                    outs[role][2][rows, column] = top

        def finish_head(head, roles):
            column = pl.ds(pl.multiple_of(head * HD, HD), HD)
            for role in roles:
                acc, total = reads[role][0][:, column], reads[role][1][:, column]
                results[role][:, column] = (acc / total).astype(BF16)

        def collect(condition):
            def add(head, count):
                chosen[count] = head
                return count + condition(table_ref[3 + head], link, far_link).astype(jnp.int32)

            return lax.fori_loop(0, heads, add, jnp.int32(0))

        for condition, items, close in cases:
            count = collect(condition)
            if items:

                def pair(step, carry, items=items, close=close):
                    take((chosen[2 * step], chosen[2 * step + 1]), items, close)
                    return carry

                lax.fori_loop(0, count // 2, pair, 0)
                pl.when(count % 2 == 1)(
                    lambda items=items, close=close, count=count: take((chosen[count - 1],), items, close)
                )
            else:

                def plain(step, carry, close=close):
                    finish_head(chosen[step], close)
                    return carry

                lax.fori_loop(0, count, plain, 0)

    operands = [table, query_tok, *sources]
    shapes = []
    aliases = {}
    if not first:
        for index, role in enumerate(names):
            if keep:
                aliases.update({len(operands) + i: 3 * index + i for i in range(3)})
            operands += list(states[role])
    if keep:
        shapes += [jax.ShapeDtypeStruct((FRAME_TOK, heads * HD), F32)] * (3 * len(names))
    for role in closed:
        if closed[role] is not None:
            aliases[len(operands)] = len(shapes)
            operands.append(closed[role])
        shapes.append(jax.ShapeDtypeStruct((FRAME_TOK, heads * HD), BF16))
    out = list(
        pl.pallas_call(
            kernel,
            out_shape=tuple(shapes),
            in_specs=[SMEM] + [VMEM] * (len(operands) - 1),
            out_specs=(VMEM,) * len(shapes),
            scratch_shapes=[pltpu.SMEM((heads + 1,), jnp.int32)],
            input_output_aliases=aliases,
            compiler_params=params(),
        )(*operands)
    )
    new_states = {role: [out.pop(0) for _ in range(3)] for role in names} if keep else {}
    return new_states, {role: out.pop(0) for role in closed}


def attend_chip(table, query_tok, edge, inner, partner_inner, partner_edge):
    order = {"E": [0, 1, 2, 3], "I": [1, 0, 2, 3]}
    reach = {"E": [1, 2, 3, 4], "I": [1, 3, 4, 4]}
    cases = [
        (
            lambda span, link, far_link, limit=limit: span == limit,
            [(role, order[role][: reach[role][limit]]) for role in "EI"],
            "",
        )
        for limit in range(4)
    ]
    return attend_step(
        table, query_tok, [edge, inner, partner_inner, partner_edge], {"E": None, "I": None}, cases, first=True
    )[0]


def attend_near(table, query_tok, state, near):
    cases = [
        (lambda span, link, far_link: (span >= 2) & link, [("E", [0]), ("I", [0])], ""),
        (lambda span, link, far_link: (span == 1) & link, [("E", [0])], ""),
    ]
    return attend_step(table, query_tok, [near], state, cases)[0]


def attend_beyond(table, query_tok, state, beyond):
    cases = [
        (lambda span, link, far_link: (span >= 3) & far_link, [("I", [0])], ""),
        (lambda span, link, far_link: (span < 3) | jnp.logical_not(link), [], "I"),
        (lambda span, link, far_link: (span < 2) | jnp.logical_not(link), [], "E"),
    ]
    return attend_step(table, query_tok, [beyond], state, cases, closed={"I": None, "E": None})


def attend_inner(table, query_tok, state, second, result):
    cases = [(lambda span, link, far_link: (span >= 3) & link, [("I", [0])], "I")]
    return attend_step(table, query_tok, [second], {"I": state}, cases, closed={"I": result})[1]["I"]


def attend_edge(table, query_tok, state, second, result):
    cases = [
        (lambda span, link, far_link: (span >= 3) & link, [("E", [0])], ""),
        (lambda span, link, far_link: (span == 2) & link, [("E", [0])], "E"),
    ]
    state, result = attend_step(table, query_tok, [second], {"E": state}, cases, closed={"E": result})
    return state["E"], result["E"]


def attend_last(table, query_tok, state, third, result):
    cases = [(lambda span, link, far_link: (span >= 3) & link, [("E", [0])], "E")]
    return attend_step(table, query_tok, [third], {"E": state}, cases, closed={"E": result})[1]["E"]


def project(attended, part, parts, out_weight, slots, received):
    groups = lax.axis_size("head")
    width = out_weight.shape[1] // groups
    rows = attended.shape[0] // parts

    def kernel(left, right, *rest):
        out = rest[-1]
        group = lax.axis_index("head")
        for index, slot in enumerate(slots):
            column = pl.ds(pl.multiple_of((group ^ slot) * width, width), width)
            sums = jnp.dot(
                left[part * rows : (part + 1) * rows, :], right[:, column], preferred_element_type=F32
            )
            for ref, (_, spots) in zip(rest, received):
                sums = sums + ref[:, spots[index] * width : (spots[index] + 1) * width].astype(F32)
            out[:, index * width : (index + 1) * width] = sums.astype(BF16)

    return pl.pallas_call(
        kernel,
        out_shape=jax.ShapeDtypeStruct((rows, len(slots) * width), BF16),
        in_specs=[VMEM] * (2 + len(received)),
        out_specs=VMEM,
        compiler_params=params(),
    )(attended, out_weight, *(array for array, _ in received))


def sum_own(attended, parts, out_weight, received):
    groups = lax.axis_size("head")
    width = out_weight.shape[1] // groups
    rows = FRAME_TOK // parts
    flat = [(array, spots[0], part) for part in range(parts) for array, spots in received[part]]

    def kernel(left, right, *rest):
        out = rest[-1]
        group = lax.axis_index("head")
        column = pl.ds(pl.multiple_of(group * width, width), width)
        sums = jnp.dot(left[...], right[:, column], preferred_element_type=F32)
        for part in range(parts):
            terms = sums[part * rows : (part + 1) * rows]
            for ref, (_, spot, owner) in zip(rest, flat):
                if owner == part:
                    terms = terms + ref[:, spot * width : (spot + 1) * width].astype(F32)
            out[part * rows : (part + 1) * rows, :] = terms

    operands = [attended, out_weight, *(array for array, _, _ in flat)]
    return pl.pallas_call(
        kernel,
        out_shape=jax.ShapeDtypeStruct((FRAME_TOK, width), F32),
        in_specs=[VMEM] * len(operands),
        out_specs=VMEM,
        compiler_params=params(),
    )(*operands)


def finish(own, received, is_edge, frames_here, into):
    parts = len(received)
    rows = FRAME_TOK // parts
    width = own.shape[1]

    def kernel(terms, *rest):
        out, buffer, sems = rest[-3:]
        parity = lax.axis_index("frame") % 2
        frame = parity if is_edge else 1 - parity
        copies = []
        for part in range(parts):
            span = slice(part * rows, (part + 1) * rows)
            buffer[span, :] = (terms[span, :] + rest[part][...].astype(F32)).astype(BF16)
            copies.append(
                pltpu.make_async_copy(
                    buffer.at[pl.ds(part * rows, rows)],
                    out.at[pl.ds(pl.multiple_of(frame * FRAME_TOK + part * rows, rows), rows)],
                    sems.at[part],
                )
            )
            copies[-1].start()
        for copy in copies:
            copy.wait()

    operands = [own, *received]
    in_specs = [VMEM] * len(operands)
    aliases = {}
    if into is not None:
        aliases = {len(operands): 0}
        operands.append(into)
        in_specs.append(HBM)
    return pl.pallas_call(
        kernel,
        out_shape=jax.ShapeDtypeStruct((frames_here * FRAME_TOK, width), BF16),
        in_specs=in_specs,
        out_specs=HBM,
        scratch_shapes=[pltpu.VMEM((FRAME_TOK, width), BF16), pltpu.SemaphoreType.DMA((parts,))],
        input_output_aliases=aliases,
        compiler_params=params(),
    )(*operands)


def body(query_tok, key_tok, value_tok, head_span, out_weight):
    frames = lax.axis_size("frame")
    groups = lax.axis_size("head")
    local_frames = key_tok.shape[0] // FRAME_TOK
    bits = groups.bit_length() - 1
    assert local_frames == 2 and frames % 2 == 0 and groups == 1 << bits and FRAME_TOK % bits == 0
    seat = lax.axis_index("frame")
    parity = seat % 2
    link = jnp.where(parity == 0, seat > 0, seat < frames - 1)
    far_link = jnp.where(parity == 0, seat < frames - 2, seat > 1)
    table = jnp.concatenate(
        [jnp.stack([parity, link, far_link]).astype(jnp.int32), head_span.astype(jnp.int32)]
    )

    def swap(value):
        return lax.ppermute(value, "frame", [(i, i ^ 1) for i in range(frames)])

    def across(value):
        pairs = [(i, i + 1) for i in range(1, frames - 1, 2)]
        return lax.ppermute(value, "frame", pairs + [(b, a) for a, b in pairs])

    edge, inner = pack_frames(key_tok, value_tok)
    near = across(edge)
    partner_inner = swap(inner)
    partner_edge = swap(edge)
    second = across(inner)
    third = across(partner_inner)
    state = attend_chip(table, query_tok, edge, inner, partner_inner, partner_edge)
    beyond = swap(near)
    state = attend_near(table, query_tok, state, near)
    state, attended = attend_beyond(table, query_tok, state, beyond)
    attended["I"] = attend_inner(table, query_tok, state["I"], second, attended["I"])

    def exchange(value, bit):
        return lax.ppermute(value, "head", [(i, i ^ (1 << bit)) for i in range(groups)])

    held = {role: [list(range(groups)) for _ in range(bits)] for role in "IE"}
    received = {role: [[] for _ in range(bits)] for role in "IE"}

    def gathered(role, part, slots):
        return [(array, [kept.index(s) for s in slots]) for array, kept in received[role][part]]

    def halve(role, stage):
        for part in range(bits):
            bit = (part + stage) % bits
            sent = [s for s in held[role][part] if s >> bit & 1]
            kept = [s for s in held[role][part] if not s >> bit & 1]
            terms = project(attended[role], part, bits, out_weight, sent, gathered(role, part, sent))
            received[role][part].append((exchange(terms, bit), kept))
            held[role][part] = kept

    halve("I", 0)
    state_e, attended["E"] = attend_edge(table, query_tok, state["E"], second, attended["E"])
    attended["E"] = attend_last(table, query_tok, state_e, third, attended["E"])
    for stage in range(bits):
        halve("E", stage)
        if stage + 1 < bits:
            halve("I", stage + 1)
    result = None
    for role in "IE":
        terms = [gathered(role, part, [0]) for part in range(bits)]
        own = sum_own(attended[role], bits, out_weight, [t[:-1] for t in terms])
        result = finish(own, [t[-1][0] for t in terms], role == "E", local_frames, result)
    return result


def solution(mesh):
    return jax.shard_map(
        body,
        mesh=mesh,
        in_specs=(
            P("frame", "head"),
            P("frame", "head"),
            P("frame", "head"),
            P("head"),
            P("head", None),
        ),
        out_specs=P("frame", "head"),
        check_vma=False,
    )
```

```python
import jax
import jax.numpy as jnp
from jax import lax
from jax.experimental import pallas as pl
from jax.experimental.pallas import tpu as pltpu
from jax.sharding import PartitionSpec as P


HD = 128
FRAME_TOK = 384
LOG2E = 1.4426950408889634
F32 = jnp.float32
BF16 = jnp.bfloat16
VMEM_LIMIT = 16 << 20
CHUNK = 384


def params():
    return pltpu.CompilerParams(vmem_limit_bytes=VMEM_LIMIT)


VMEM = pl.BlockSpec(memory_space=pltpu.VMEM)
SMEM = pl.BlockSpec(memory_space=pltpu.SMEM)
HBM = pl.BlockSpec(memory_space=pltpu.HBM)


def pack_frames(key_tok, value_tok):
    parity = lax.axis_index("frame") % 2

    def packed(key, value, frame):
        rows = [lax.dynamic_slice_in_dim(array, frame * FRAME_TOK, FRAME_TOK, 0) for array in (key, value)]
        return jnp.concatenate(rows, axis=0)

    edge = packed(key_tok, value_tok, parity)
    edge, key_tok, value_tok = lax.optimization_barrier((edge, key_tok, value_tok))
    return edge, packed(key_tok, value_tok, 1 - parity)


def attend_step(head_span, query_tok, sources, states, cases, first=False, closed=None):
    heads = query_tok.shape[1] // HD
    frames = lax.axis_size("frame")
    names = list(states)
    closed = closed or {}
    scale = LOG2E / HD**0.5
    keep = first or any(items and not close for _, items, close in cases)

    def kernel(span_ref, query, *refs):
        refs = list(refs)
        chosen = refs.pop()
        loaded = [refs.pop(0) for _ in sources]
        olds = {} if first else {role: [refs.pop(0) for _ in range(3)] for role in names}
        for role in closed:
            if closed[role] is not None:
                refs.pop(0)
        outs = {role: [refs.pop(0) for _ in range(3)] for role in names} if keep else {}
        results = {role: refs.pop(0) for role in closed}
        reads = outs if keep and not first else olds
        seat = lax.axis_index("frame")
        parity = seat % 2
        link = ((parity == 0) & (seat > 0)) | ((parity == 1) & (seat < frames - 1))
        far_link = ((parity == 0) & (seat < frames - 2)) | ((parity == 1) & (seat > 1))
        starts = {"E": parity * FRAME_TOK, "I": (1 - parity) * FRAME_TOK}

        def wide(tops, times):
            return jnp.concatenate([tops] * times, axis=1)

        def take(heads_now, items, close):
            work = []
            for head in heads_now:
                column = pl.ds(pl.multiple_of(head * HD, HD), HD)
                for role, picked in items:
                    keys = jnp.concatenate([loaded[i][:FRAME_TOK, column] for i in picked], axis=0)
                    values = jnp.concatenate([loaded[i][FRAME_TOK:, column] for i in picked], axis=0)
                    values = jnp.concatenate([values, jnp.ones_like(values)], axis=1)
                    for at in range(0, FRAME_TOK, CHUNK):
                        work.append((role, column, slice(at, at + CHUNK), keys, values, len(picked)))
            done = []
            for role, column, rows, keys, values, count in work:
                here = pl.ds(pl.multiple_of(starts[role] + rows.start, CHUNK), CHUNK)
                scores = lax.dot_general(
                    query[here, column], keys, (((1,), (1,)), ((), ())), preferred_element_type=F32
                )
                top = jnp.broadcast_to(jnp.max(scores, axis=1, keepdims=True), (CHUNK, HD))
                fade = None
                if not first:
                    old_top = reads[role][2][rows, column]
                    top = jnp.maximum(top, old_top)
                    fade = jnp.exp2((old_top - top) * scale)
                times = count * FRAME_TOK // HD
                weights = jnp.exp2((scores - wide(top, times)) * scale).astype(BF16)
                mixed = jnp.dot(weights, values, preferred_element_type=F32)
                done.append((role, column, rows, mixed, top, fade))
            for role, column, rows, mixed, top, fade in done:
                acc, total = mixed[:, :HD], mixed[:, HD:]
                if not first:
                    acc = reads[role][0][rows, column] * fade + acc
                    total = reads[role][1][rows, column] * fade + total
                if role in close:
                    results[role][rows, column] = (acc / total).astype(BF16)
                else:
                    outs[role][0][rows, column] = acc
                    outs[role][1][rows, column] = total
                    outs[role][2][rows, column] = top

        def finish_head(head, roles):
            column = pl.ds(pl.multiple_of(head * HD, HD), HD)
            for role in roles:
                acc, total = reads[role][0][:, column], reads[role][1][:, column]
                results[role][:, column] = (acc / total).astype(BF16)

        def collect(condition):
            def add(head, count):
                chosen[count] = head
                return count + condition(span_ref[head], link, far_link).astype(jnp.int32)

            return lax.fori_loop(0, heads, add, jnp.int32(0))

        for condition, items, close in cases:
            count = collect(condition)
            if items:

                def pair(step, carry, items=items, close=close):
                    take((chosen[2 * step], chosen[2 * step + 1]), items, close)
                    return carry

                lax.fori_loop(0, count // 2, pair, 0)
                pl.when(count % 2 == 1)(
                    lambda items=items, close=close, count=count: take((chosen[count - 1],), items, close)
                )
            else:

                def plain(step, carry, close=close):
                    finish_head(chosen[step], close)
                    return carry

                lax.fori_loop(0, count, plain, 0)

    operands = [head_span, query_tok, *sources]
    shapes = []
    aliases = {}
    if not first:
        for index, role in enumerate(names):
            if keep:
                aliases.update({len(operands) + i: 3 * index + i for i in range(3)})
            operands += list(states[role])
    if keep:
        shapes += [jax.ShapeDtypeStruct((FRAME_TOK, heads * HD), F32)] * (3 * len(names))
    for role in closed:
        if closed[role] is not None:
            aliases[len(operands)] = len(shapes)
            operands.append(closed[role])
        shapes.append(jax.ShapeDtypeStruct((FRAME_TOK, heads * HD), BF16))
    out = list(
        pl.pallas_call(
            kernel,
            out_shape=tuple(shapes),
            in_specs=[SMEM] + [VMEM] * (len(operands) - 1),
            out_specs=(VMEM,) * len(shapes),
            scratch_shapes=[pltpu.SMEM((heads + 1,), jnp.int32)],
            input_output_aliases=aliases,
            compiler_params=params(),
        )(*operands)
    )
    new_states = {role: [out.pop(0) for _ in range(3)] for role in names} if keep else {}
    return new_states, {role: out.pop(0) for role in closed}


def attend_chip(head_span, query_tok, edge, inner, partner_inner, partner_edge):
    order = {"E": [0, 1, 2, 3], "I": [1, 0, 2, 3]}
    reach = {"E": [1, 2, 3, 4], "I": [1, 3, 4, 4]}
    cases = [
        (
            lambda span, link, far_link, limit=limit: span == limit,
            [(role, order[role][: reach[role][limit]]) for role in "EI"],
            "",
        )
        for limit in range(4)
    ]
    return attend_step(
        head_span, query_tok, [edge, inner, partner_inner, partner_edge], {"E": None, "I": None}, cases, first=True
    )[0]


def attend_near(head_span, query_tok, state, near):
    cases = [
        (lambda span, link, far_link: (span >= 2) & link, [("E", [0]), ("I", [0])], ""),
        (lambda span, link, far_link: (span == 1) & link, [("E", [0])], ""),
    ]
    return attend_step(head_span, query_tok, [near], state, cases)[0]


def attend_beyond(head_span, query_tok, state, beyond):
    cases = [
        (lambda span, link, far_link: (span >= 3) & far_link, [("I", [0])], ""),
        (lambda span, link, far_link: (span < 3) | jnp.logical_not(link), [], "I"),
        (lambda span, link, far_link: (span < 2) | jnp.logical_not(link), [], "E"),
    ]
    return attend_step(head_span, query_tok, [beyond], state, cases, closed={"I": None, "E": None})


def attend_inner(head_span, query_tok, state, second, result):
    cases = [(lambda span, link, far_link: (span >= 3) & link, [("I", [0])], "I")]
    return attend_step(head_span, query_tok, [second], {"I": state}, cases, closed={"I": result})[1]["I"]


def attend_edge(head_span, query_tok, state, second, result):
    cases = [
        (lambda span, link, far_link: (span >= 3) & link, [("E", [0])], ""),
        (lambda span, link, far_link: (span == 2) & link, [("E", [0])], "E"),
    ]
    state, result = attend_step(head_span, query_tok, [second], {"E": state}, cases, closed={"E": result})
    return state["E"], result["E"]


def attend_last(head_span, query_tok, state, third, result):
    cases = [(lambda span, link, far_link: (span >= 3) & link, [("E", [0])], "E")]
    return attend_step(head_span, query_tok, [third], {"E": state}, cases, closed={"E": result})[1]["E"]


def project(attended, part, parts, out_weight, slots, received):
    groups = lax.axis_size("head")
    width = out_weight.shape[1] // groups
    rows = attended.shape[0] // parts

    def kernel(left, right, *rest):
        out = rest[-1]
        group = lax.axis_index("head")
        for index, slot in enumerate(slots):
            column = pl.ds(pl.multiple_of((group ^ slot) * width, width), width)
            sums = jnp.dot(
                left[part * rows : (part + 1) * rows, :], right[:, column], preferred_element_type=F32
            )
            for ref, (_, spots) in zip(rest, received):
                sums = sums + ref[:, spots[index] * width : (spots[index] + 1) * width].astype(F32)
            out[:, index * width : (index + 1) * width] = sums.astype(BF16)

    return pl.pallas_call(
        kernel,
        out_shape=jax.ShapeDtypeStruct((rows, len(slots) * width), BF16),
        in_specs=[VMEM] * (2 + len(received)),
        out_specs=VMEM,
        compiler_params=params(),
    )(attended, out_weight, *(array for array, _ in received))


def sum_own(attended, parts, out_weight, received):
    groups = lax.axis_size("head")
    width = out_weight.shape[1] // groups
    rows = FRAME_TOK // parts
    flat = [(array, spots[0], part) for part in range(parts) for array, spots in received[part]]

    def kernel(left, right, *rest):
        out = rest[-1]
        group = lax.axis_index("head")
        column = pl.ds(pl.multiple_of(group * width, width), width)
        sums = jnp.dot(left[...], right[:, column], preferred_element_type=F32)
        for part in range(parts):
            terms = sums[part * rows : (part + 1) * rows]
            for ref, (_, spot, owner) in zip(rest, flat):
                if owner == part:
                    terms = terms + ref[:, spot * width : (spot + 1) * width].astype(F32)
            out[part * rows : (part + 1) * rows, :] = terms

    operands = [attended, out_weight, *(array for array, _, _ in flat)]
    return pl.pallas_call(
        kernel,
        out_shape=jax.ShapeDtypeStruct((FRAME_TOK, width), F32),
        in_specs=[VMEM] * len(operands),
        out_specs=VMEM,
        compiler_params=params(),
    )(*operands)


def finish(own, received, is_edge, frames_here, into):
    parts = len(received)
    rows = FRAME_TOK // parts
    width = own.shape[1]

    def kernel(terms, *rest):
        out, buffer, sems = rest[-3:]
        parity = lax.axis_index("frame") % 2
        frame = parity if is_edge else 1 - parity
        copies = []
        for part in range(parts):
            span = slice(part * rows, (part + 1) * rows)
            buffer[span, :] = (terms[span, :] + rest[part][...].astype(F32)).astype(BF16)
            copies.append(
                pltpu.make_async_copy(
                    buffer.at[pl.ds(part * rows, rows)],
                    out.at[pl.ds(pl.multiple_of(frame * FRAME_TOK + part * rows, rows), rows)],
                    sems.at[part],
                )
            )
            copies[-1].start()
        for copy in copies:
            copy.wait()

    operands = [own, *received]
    in_specs = [VMEM] * len(operands)
    aliases = {}
    if into is not None:
        aliases = {len(operands): 0}
        operands.append(into)
        in_specs.append(HBM)
    return pl.pallas_call(
        kernel,
        out_shape=jax.ShapeDtypeStruct((frames_here * FRAME_TOK, width), BF16),
        in_specs=in_specs,
        out_specs=HBM,
        scratch_shapes=[pltpu.VMEM((FRAME_TOK, width), BF16), pltpu.SemaphoreType.DMA((parts,))],
        input_output_aliases=aliases,
        compiler_params=params(),
    )(*operands)


def body(query_tok, key_tok, value_tok, head_span, out_weight):
    frames = lax.axis_size("frame")
    groups = lax.axis_size("head")
    local_frames = key_tok.shape[0] // FRAME_TOK
    bits = groups.bit_length() - 1
    assert local_frames == 2 and frames % 2 == 0 and groups == 1 << bits and FRAME_TOK % bits == 0

    def swap(value):
        return lax.ppermute(value, "frame", [(i, i ^ 1) for i in range(frames)])

    def across(value):
        pairs = [(i, i + 1) for i in range(1, frames - 1, 2)]
        return lax.ppermute(value, "frame", pairs + [(b, a) for a, b in pairs])

    edge, inner = pack_frames(key_tok, value_tok)
    near = across(edge)
    partner_inner = swap(inner)
    partner_edge = swap(edge)
    second = across(inner)
    third = across(partner_inner)
    state = attend_chip(head_span, query_tok, edge, inner, partner_inner, partner_edge)
    beyond = swap(near)
    state = attend_near(head_span, query_tok, state, near)
    state, attended = attend_beyond(head_span, query_tok, state, beyond)
    attended["I"] = attend_inner(head_span, query_tok, state["I"], second, attended["I"])

    def exchange(value, bit):
        return lax.ppermute(value, "head", [(i, i ^ (1 << bit)) for i in range(groups)])

    held = {role: [list(range(groups)) for _ in range(bits)] for role in "IE"}
    received = {role: [[] for _ in range(bits)] for role in "IE"}

    def gathered(role, part, slots):
        return [(array, [kept.index(s) for s in slots]) for array, kept in received[role][part]]

    def halve(role, stage):
        for part in range(bits):
            bit = (part + stage) % bits
            sent = [s for s in held[role][part] if s >> bit & 1]
            kept = [s for s in held[role][part] if not s >> bit & 1]
            terms = project(attended[role], part, bits, out_weight, sent, gathered(role, part, sent))
            received[role][part].append((exchange(terms, bit), kept))
            held[role][part] = kept

    halve("I", 0)
    state_e, attended["E"] = attend_edge(head_span, query_tok, state["E"], second, attended["E"])
    attended["E"] = attend_last(head_span, query_tok, state_e, third, attended["E"])
    for stage in range(bits):
        halve("E", stage)
        if stage + 1 < bits:
            halve("I", stage + 1)
    result = None
    for role in "IE":
        terms = [gathered(role, part, [0]) for part in range(bits)]
        own = sum_own(attended[role], bits, out_weight, [t[:-1] for t in terms])
        result = finish(own, [t[-1][0] for t in terms], role == "E", local_frames, result)
    return result


def solution(mesh):
    return jax.shard_map(
        body,
        mesh=mesh,
        in_specs=(
            P("frame", "head"),
            P("frame", "head"),
            P("frame", "head"),
            P("head"),
            P("head", None),
        ),
        out_specs=P("frame", "head"),
        check_vma=False,
    )
```

```python
import jax
import jax.numpy as jnp
from jax import lax
from jax.experimental import pallas as pl
from jax.experimental.pallas import tpu as pltpu
from jax.sharding import PartitionSpec as P


HD = 128
FRAME_TOK = 384
LOG2E = 1.4426950408889634
F32 = jnp.float32
BF16 = jnp.bfloat16
VMEM_LIMIT = 16 << 20
CHUNK = 384
LEAN = 16


def params():
    return pltpu.CompilerParams(vmem_limit_bytes=VMEM_LIMIT)


VMEM = pl.BlockSpec(memory_space=pltpu.VMEM)
SMEM = pl.BlockSpec(memory_space=pltpu.SMEM)
HBM = pl.BlockSpec(memory_space=pltpu.HBM)


def pack_frames(key_tok, value_tok):
    parity = lax.axis_index("frame") % 2

    def packed(key, value, frame):
        rows = [lax.dynamic_slice_in_dim(array, frame * FRAME_TOK, FRAME_TOK, 0) for array in (key, value)]
        return jnp.concatenate(rows, axis=0)

    edge = packed(key_tok, value_tok, parity)
    edge, key_tok, value_tok = lax.optimization_barrier((edge, key_tok, value_tok))
    return edge, packed(key_tok, value_tok, 1 - parity)


def attend_step(head_span, query_tok, sources, states, cases, first=False, closed=None):
    heads = query_tok.shape[1] // HD
    frames = lax.axis_size("frame")
    names = list(states)
    closed = closed or {}
    scale = LOG2E / HD**0.5
    keep = first or any(items and not close for _, items, close in cases)

    def kernel(span_ref, query, *refs):
        refs = list(refs)
        chosen = refs.pop()
        loaded = [refs.pop(0) for _ in sources]
        olds = {} if first else {role: [refs.pop(0) for _ in range(3)] for role in names}
        for role in closed:
            if closed[role] is not None:
                refs.pop(0)
        outs = {role: [refs.pop(0) for _ in range(3)] for role in names} if keep else {}
        results = {role: refs.pop(0) for role in closed}
        reads = outs if keep and not first else olds
        seat = lax.axis_index("frame")
        parity = seat % 2
        link = ((parity == 0) & (seat > 0)) | ((parity == 1) & (seat < frames - 1))
        far_link = ((parity == 0) & (seat < frames - 2)) | ((parity == 1) & (seat > 1))
        starts = {"E": parity * FRAME_TOK, "I": (1 - parity) * FRAME_TOK}

        def wide(tops, times):
            return jnp.concatenate([tops] * times, axis=1)

        def take(heads_now, items, close):
            work = []
            for head in heads_now:
                column = pl.ds(pl.multiple_of(head * HD, HD), HD)
                for role, picked in items:
                    keys = jnp.concatenate([loaded[i][:FRAME_TOK, column] for i in picked], axis=0)
                    values = jnp.concatenate([loaded[i][FRAME_TOK:, column] for i in picked], axis=0)
                    values = jnp.concatenate([values, jnp.ones_like(values)], axis=1)
                    for at in range(0, FRAME_TOK, CHUNK):
                        work.append((role, column, slice(at, at + CHUNK), keys, values, len(picked)))
            done = []
            for role, column, rows, keys, values, count in work:
                here = pl.ds(pl.multiple_of(starts[role] + rows.start, CHUNK), CHUNK)
                scores = lax.dot_general(
                    query[here, column], keys, (((1,), (1,)), ((), ())), preferred_element_type=F32
                )
                top = jnp.broadcast_to(jnp.max(scores, axis=1, keepdims=True), (CHUNK, HD))
                fade = None
                if not first:
                    old_top = reads[role][2][rows, column]
                    top = jnp.maximum(top, old_top)
                    fade = jnp.exp2((old_top - top) * scale)
                times = count * FRAME_TOK // HD
                weights = jnp.exp2((scores - wide(top, times)) * scale).astype(BF16)
                mixed = jnp.dot(weights, values, preferred_element_type=F32)
                done.append((role, column, rows, mixed, top, fade))
            for role, column, rows, mixed, top, fade in done:
                acc, total = mixed[:, :HD], mixed[:, HD:]
                if not first:
                    acc = reads[role][0][rows, column] * fade + acc
                    total = reads[role][1][rows, column] * fade + total
                if role in close:
                    results[role][rows, column] = (acc / total).astype(BF16)
                else:
                    outs[role][0][rows, column] = acc
                    outs[role][1][rows, column] = total
                    outs[role][2][rows, column] = top

        def finish_head(head, roles):
            column = pl.ds(pl.multiple_of(head * HD, HD), HD)
            for role in roles:
                acc, total = reads[role][0][:, column], reads[role][1][:, column]
                results[role][:, column] = (acc / total).astype(BF16)

        def collect(condition):
            def add(head, count):
                chosen[count] = head
                return count + condition(span_ref[head], link, far_link).astype(jnp.int32)

            return lax.fori_loop(0, heads, add, jnp.int32(0))

        for condition, items, close in cases:
            count = collect(condition)
            if items:

                def pair(step, carry, items=items, close=close):
                    take((chosen[2 * step], chosen[2 * step + 1]), items, close)
                    return carry

                lax.fori_loop(0, count // 2, pair, 0)
                pl.when(count % 2 == 1)(
                    lambda items=items, close=close, count=count: take((chosen[count - 1],), items, close)
                )
            else:

                def plain(step, carry, close=close):
                    finish_head(chosen[step], close)
                    return carry

                lax.fori_loop(0, count, plain, 0)

    operands = [head_span, query_tok, *sources]
    shapes = []
    aliases = {}
    if not first:
        for index, role in enumerate(names):
            if keep:
                aliases.update({len(operands) + i: 3 * index + i for i in range(3)})
            operands += list(states[role])
    if keep:
        shapes += [jax.ShapeDtypeStruct((FRAME_TOK, heads * HD), F32)] * (3 * len(names))
    for role in closed:
        if closed[role] is not None:
            aliases[len(operands)] = len(shapes)
            operands.append(closed[role])
        shapes.append(jax.ShapeDtypeStruct((FRAME_TOK, heads * HD), BF16))
    out = list(
        pl.pallas_call(
            kernel,
            out_shape=tuple(shapes),
            in_specs=[SMEM] + [VMEM] * (len(operands) - 1),
            out_specs=(VMEM,) * len(shapes),
            scratch_shapes=[pltpu.SMEM((heads + 1,), jnp.int32)],
            input_output_aliases=aliases,
            compiler_params=params(),
        )(*operands)
    )
    new_states = {role: [out.pop(0) for _ in range(3)] for role in names} if keep else {}
    return new_states, {role: out.pop(0) for role in closed}


def attend_chip(head_span, query_tok, edge, inner, partner_inner, partner_edge):
    order = {"E": [0, 1, 2, 3], "I": [1, 0, 2, 3]}
    reach = {"E": [1, 2, 3, 4], "I": [1, 3, 4, 4]}
    cases = [
        (
            lambda span, link, far_link, limit=limit: span == limit,
            [(role, order[role][: reach[role][limit]]) for role in "EI"],
            "",
        )
        for limit in range(4)
    ]
    return attend_step(
        head_span, query_tok, [edge, inner, partner_inner, partner_edge], {"E": None, "I": None}, cases, first=True
    )[0]


def attend_near(head_span, query_tok, state, near):
    cases = [
        (lambda span, link, far_link: (span >= 2) & link, [("E", [0]), ("I", [0])], ""),
        (lambda span, link, far_link: (span == 1) & link, [("E", [0])], ""),
    ]
    return attend_step(head_span, query_tok, [near], state, cases)[0]


def attend_beyond(head_span, query_tok, state, beyond):
    cases = [
        (lambda span, link, far_link: (span >= 3) & far_link, [("I", [0])], ""),
        (lambda span, link, far_link: (span < 3) | jnp.logical_not(link), [], "I"),
        (lambda span, link, far_link: (span < 2) | jnp.logical_not(link), [], "E"),
    ]
    return attend_step(head_span, query_tok, [beyond], state, cases, closed={"I": None, "E": None})


def attend_inner(head_span, query_tok, state, second, result):
    cases = [(lambda span, link, far_link: (span >= 3) & link, [("I", [0])], "I")]
    return attend_step(head_span, query_tok, [second], {"I": state}, cases, closed={"I": result})[1]["I"]


def attend_edge(head_span, query_tok, state, second, result):
    cases = [
        (lambda span, link, far_link: (span >= 3) & link, [("E", [0])], ""),
        (lambda span, link, far_link: (span == 2) & link, [("E", [0])], "E"),
    ]
    state, result = attend_step(head_span, query_tok, [second], {"E": state}, cases, closed={"E": result})
    return state["E"], result["E"]


def attend_last(head_span, query_tok, state, third, result):
    cases = [(lambda span, link, far_link: (span >= 3) & link, [("E", [0])], "E")]
    return attend_step(head_span, query_tok, [third], {"E": state}, cases, closed={"E": result})[1]["E"]


def row_edges(parts):
    return [0] + [part * FRAME_TOK // parts + LEAN for part in range(1, parts)] + [FRAME_TOK]


def project(attended, part, parts, out_weight, slots, received):
    groups = lax.axis_size("head")
    width = out_weight.shape[1] // groups
    start, stop = row_edges(parts)[part : part + 2]
    rows = stop - start

    def kernel(left, right, *rest):
        out = rest[-1]
        group = lax.axis_index("head")
        for index, slot in enumerate(slots):
            column = pl.ds(pl.multiple_of((group ^ slot) * width, width), width)
            sums = jnp.dot(
                left[start:stop, :], right[:, column], preferred_element_type=F32
            )
            for ref, (_, spots) in zip(rest, received):
                sums = sums + ref[:, spots[index] * width : (spots[index] + 1) * width].astype(F32)
            out[:, index * width : (index + 1) * width] = sums.astype(BF16)

    return pl.pallas_call(
        kernel,
        out_shape=jax.ShapeDtypeStruct((rows, len(slots) * width), BF16),
        in_specs=[VMEM] * (2 + len(received)),
        out_specs=VMEM,
        compiler_params=params(),
    )(attended, out_weight, *(array for array, _ in received))


def sum_own(attended, parts, out_weight, received):
    groups = lax.axis_size("head")
    width = out_weight.shape[1] // groups
    edges = row_edges(parts)
    flat = [(array, spots[0], part) for part in range(parts) for array, spots in received[part]]

    def kernel(left, right, *rest):
        out = rest[-1]
        group = lax.axis_index("head")
        column = pl.ds(pl.multiple_of(group * width, width), width)
        sums = jnp.dot(left[...], right[:, column], preferred_element_type=F32)
        for part in range(parts):
            terms = sums[edges[part] : edges[part + 1]]
            for ref, (_, spot, owner) in zip(rest, flat):
                if owner == part:
                    terms = terms + ref[:, spot * width : (spot + 1) * width].astype(F32)
            out[edges[part] : edges[part + 1], :] = terms

    operands = [attended, out_weight, *(array for array, _, _ in flat)]
    return pl.pallas_call(
        kernel,
        out_shape=jax.ShapeDtypeStruct((FRAME_TOK, width), F32),
        in_specs=[VMEM] * len(operands),
        out_specs=VMEM,
        compiler_params=params(),
    )(*operands)


def finish(own, received, is_edge, frames_here, into):
    parts = len(received)
    edges = row_edges(parts)
    width = own.shape[1]

    def kernel(terms, *rest):
        out, buffer, sems = rest[-3:]
        parity = lax.axis_index("frame") % 2
        frame = parity if is_edge else 1 - parity
        copies = []
        for part in range(parts):
            start, rows = edges[part], edges[part + 1] - edges[part]
            span = slice(start, start + rows)
            buffer[span, :] = (terms[span, :] + rest[part][...].astype(F32)).astype(BF16)
            copies.append(
                pltpu.make_async_copy(
                    buffer.at[pl.ds(start, rows)],
                    out.at[pl.ds(pl.multiple_of(frame * FRAME_TOK + start, 16), rows)],
                    sems.at[part],
                )
            )
            copies[-1].start()
        for copy in copies:
            copy.wait()

    operands = [own, *received]
    in_specs = [VMEM] * len(operands)
    aliases = {}
    if into is not None:
        aliases = {len(operands): 0}
        operands.append(into)
        in_specs.append(HBM)
    return pl.pallas_call(
        kernel,
        out_shape=jax.ShapeDtypeStruct((frames_here * FRAME_TOK, width), BF16),
        in_specs=in_specs,
        out_specs=HBM,
        scratch_shapes=[pltpu.VMEM((FRAME_TOK, width), BF16), pltpu.SemaphoreType.DMA((parts,))],
        input_output_aliases=aliases,
        compiler_params=params(),
    )(*operands)


def body(query_tok, key_tok, value_tok, head_span, out_weight):
    frames = lax.axis_size("frame")
    groups = lax.axis_size("head")
    local_frames = key_tok.shape[0] // FRAME_TOK
    bits = groups.bit_length() - 1
    assert local_frames == 2 and frames % 2 == 0 and groups == 1 << bits and FRAME_TOK % bits == 0

    def swap(value):
        return lax.ppermute(value, "frame", [(i, i ^ 1) for i in range(frames)])

    def across(value):
        pairs = [(i, i + 1) for i in range(1, frames - 1, 2)]
        return lax.ppermute(value, "frame", pairs + [(b, a) for a, b in pairs])

    edge, inner = pack_frames(key_tok, value_tok)
    near = across(edge)
    partner_inner = swap(inner)
    partner_edge = swap(edge)
    second = across(inner)
    third = across(partner_inner)
    state = attend_chip(head_span, query_tok, edge, inner, partner_inner, partner_edge)
    beyond = swap(near)
    state = attend_near(head_span, query_tok, state, near)
    state, attended = attend_beyond(head_span, query_tok, state, beyond)
    attended["I"] = attend_inner(head_span, query_tok, state["I"], second, attended["I"])

    def exchange(value, bit):
        return lax.ppermute(value, "head", [(i, i ^ (1 << bit)) for i in range(groups)])

    held = {role: [list(range(groups)) for _ in range(bits)] for role in "IE"}
    received = {role: [[] for _ in range(bits)] for role in "IE"}

    def gathered(role, part, slots):
        return [(array, [kept.index(s) for s in slots]) for array, kept in received[role][part]]

    def halve(role, stage):
        for part in range(bits):
            bit = (part + stage) % bits
            sent = [s for s in held[role][part] if s >> bit & 1]
            kept = [s for s in held[role][part] if not s >> bit & 1]
            terms = project(attended[role], part, bits, out_weight, sent, gathered(role, part, sent))
            received[role][part].append((exchange(terms, bit), kept))
            held[role][part] = kept

    halve("I", 0)
    state_e, attended["E"] = attend_edge(head_span, query_tok, state["E"], second, attended["E"])
    attended["E"] = attend_last(head_span, query_tok, state_e, third, attended["E"])
    for stage in range(bits):
        halve("E", stage)
        if stage + 1 < bits:
            halve("I", stage + 1)
    result = None
    for role in "IE":
        terms = [gathered(role, part, [0]) for part in range(bits)]
        own = sum_own(attended[role], bits, out_weight, [t[:-1] for t in terms])
        result = finish(own, [t[-1][0] for t in terms], role == "E", local_frames, result)
    return result


def solution(mesh):
    return jax.shard_map(
        body,
        mesh=mesh,
        in_specs=(
            P("frame", "head"),
            P("frame", "head"),
            P("frame", "head"),
            P("head"),
            P("head", None),
        ),
        out_specs=P("frame", "head"),
        check_vma=False,
    )
```

```python
import jax
import jax.numpy as jnp
from jax import lax
from jax.experimental import pallas as pl
from jax.experimental.pallas import tpu as pltpu
from jax.sharding import PartitionSpec as P


HD = 128
FRAME_TOK = 384
LOG2E = 1.4426950408889634
F32 = jnp.float32
BF16 = jnp.bfloat16
VMEM_LIMIT = 16 << 20
CHUNK = 384
LEAN = 32


def params():
    return pltpu.CompilerParams(vmem_limit_bytes=VMEM_LIMIT)


VMEM = pl.BlockSpec(memory_space=pltpu.VMEM)
SMEM = pl.BlockSpec(memory_space=pltpu.SMEM)
HBM = pl.BlockSpec(memory_space=pltpu.HBM)


def pack_frames(key_tok, value_tok):
    parity = lax.axis_index("frame") % 2

    def packed(key, value, frame):
        rows = [lax.dynamic_slice_in_dim(array, frame * FRAME_TOK, FRAME_TOK, 0) for array in (key, value)]
        return jnp.concatenate(rows, axis=0)

    edge = packed(key_tok, value_tok, parity)
    edge, key_tok, value_tok = lax.optimization_barrier((edge, key_tok, value_tok))
    return edge, packed(key_tok, value_tok, 1 - parity)


def attend_step(head_span, query_tok, sources, states, cases, first=False, closed=None):
    heads = query_tok.shape[1] // HD
    frames = lax.axis_size("frame")
    names = list(states)
    closed = closed or {}
    scale = LOG2E / HD**0.5
    keep = first or any(items and not close for _, items, close in cases)

    def kernel(span_ref, query, *refs):
        refs = list(refs)
        chosen = refs.pop()
        loaded = [refs.pop(0) for _ in sources]
        olds = {} if first else {role: [refs.pop(0) for _ in range(3)] for role in names}
        for role in closed:
            if closed[role] is not None:
                refs.pop(0)
        outs = {role: [refs.pop(0) for _ in range(3)] for role in names} if keep else {}
        results = {role: refs.pop(0) for role in closed}
        reads = outs if keep and not first else olds
        seat = lax.axis_index("frame")
        parity = seat % 2
        link = ((parity == 0) & (seat > 0)) | ((parity == 1) & (seat < frames - 1))
        far_link = ((parity == 0) & (seat < frames - 2)) | ((parity == 1) & (seat > 1))
        starts = {"E": parity * FRAME_TOK, "I": (1 - parity) * FRAME_TOK}

        def wide(tops, times):
            return jnp.concatenate([tops] * times, axis=1)

        def take(heads_now, items, close):
            work = []
            for head in heads_now:
                column = pl.ds(pl.multiple_of(head * HD, HD), HD)
                for role, picked in items:
                    keys = jnp.concatenate([loaded[i][:FRAME_TOK, column] for i in picked], axis=0)
                    values = jnp.concatenate([loaded[i][FRAME_TOK:, column] for i in picked], axis=0)
                    values = jnp.concatenate([values, jnp.ones_like(values)], axis=1)
                    for at in range(0, FRAME_TOK, CHUNK):
                        work.append((role, column, slice(at, at + CHUNK), keys, values, len(picked)))
            done = []
            for role, column, rows, keys, values, count in work:
                here = pl.ds(pl.multiple_of(starts[role] + rows.start, CHUNK), CHUNK)
                scores = lax.dot_general(
                    query[here, column], keys, (((1,), (1,)), ((), ())), preferred_element_type=F32
                )
                top = jnp.broadcast_to(jnp.max(scores, axis=1, keepdims=True), (CHUNK, HD))
                fade = None
                if not first:
                    old_top = reads[role][2][rows, column]
                    top = jnp.maximum(top, old_top)
                    fade = jnp.exp2((old_top - top) * scale)
                times = count * FRAME_TOK // HD
                weights = jnp.exp2((scores - wide(top, times)) * scale).astype(BF16)
                mixed = jnp.dot(weights, values, preferred_element_type=F32)
                done.append((role, column, rows, mixed, top, fade))
            for role, column, rows, mixed, top, fade in done:
                acc, total = mixed[:, :HD], mixed[:, HD:]
                if not first:
                    acc = reads[role][0][rows, column] * fade + acc
                    total = reads[role][1][rows, column] * fade + total
                if role in close:
                    results[role][rows, column] = (acc / total).astype(BF16)
                else:
                    outs[role][0][rows, column] = acc
                    outs[role][1][rows, column] = total
                    outs[role][2][rows, column] = top

        def finish_head(head, roles):
            column = pl.ds(pl.multiple_of(head * HD, HD), HD)
            for role in roles:
                acc, total = reads[role][0][:, column], reads[role][1][:, column]
                results[role][:, column] = (acc / total).astype(BF16)

        def collect(condition):
            def add(head, count):
                chosen[count] = head
                return count + condition(span_ref[head], link, far_link).astype(jnp.int32)

            return lax.fori_loop(0, heads, add, jnp.int32(0))

        for condition, items, close in cases:
            count = collect(condition)
            if items:

                def pair(step, carry, items=items, close=close):
                    take((chosen[2 * step], chosen[2 * step + 1]), items, close)
                    return carry

                lax.fori_loop(0, count // 2, pair, 0)
                pl.when(count % 2 == 1)(
                    lambda items=items, close=close, count=count: take((chosen[count - 1],), items, close)
                )
            else:

                def plain(step, carry, close=close):
                    finish_head(chosen[step], close)
                    return carry

                lax.fori_loop(0, count, plain, 0)

    operands = [head_span, query_tok, *sources]
    shapes = []
    aliases = {}
    if not first:
        for index, role in enumerate(names):
            if keep:
                aliases.update({len(operands) + i: 3 * index + i for i in range(3)})
            operands += list(states[role])
    if keep:
        shapes += [jax.ShapeDtypeStruct((FRAME_TOK, heads * HD), F32)] * (3 * len(names))
    for role in closed:
        if closed[role] is not None:
            aliases[len(operands)] = len(shapes)
            operands.append(closed[role])
        shapes.append(jax.ShapeDtypeStruct((FRAME_TOK, heads * HD), BF16))
    out = list(
        pl.pallas_call(
            kernel,
            out_shape=tuple(shapes),
            in_specs=[SMEM] + [VMEM] * (len(operands) - 1),
            out_specs=(VMEM,) * len(shapes),
            scratch_shapes=[pltpu.SMEM((heads + 1,), jnp.int32)],
            input_output_aliases=aliases,
            compiler_params=params(),
        )(*operands)
    )
    new_states = {role: [out.pop(0) for _ in range(3)] for role in names} if keep else {}
    return new_states, {role: out.pop(0) for role in closed}


def attend_chip(head_span, query_tok, edge, inner, partner_inner, partner_edge):
    order = {"E": [0, 1, 2, 3], "I": [1, 0, 2, 3]}
    reach = {"E": [1, 2, 3, 4], "I": [1, 3, 4, 4]}
    cases = [
        (
            lambda span, link, far_link, limit=limit: span == limit,
            [(role, order[role][: reach[role][limit]]) for role in "EI"],
            "",
        )
        for limit in range(4)
    ]
    return attend_step(
        head_span, query_tok, [edge, inner, partner_inner, partner_edge], {"E": None, "I": None}, cases, first=True
    )[0]


def attend_near(head_span, query_tok, state, near):
    cases = [
        (lambda span, link, far_link: (span >= 2) & link, [("E", [0]), ("I", [0])], ""),
        (lambda span, link, far_link: (span == 1) & link, [("E", [0])], ""),
    ]
    return attend_step(head_span, query_tok, [near], state, cases)[0]


def attend_beyond(head_span, query_tok, state, beyond):
    cases = [
        (lambda span, link, far_link: (span >= 3) & far_link, [("I", [0])], ""),
        (lambda span, link, far_link: (span < 3) | jnp.logical_not(link), [], "I"),
        (lambda span, link, far_link: (span < 2) | jnp.logical_not(link), [], "E"),
    ]
    return attend_step(head_span, query_tok, [beyond], state, cases, closed={"I": None, "E": None})


def attend_inner(head_span, query_tok, state, second, result):
    cases = [(lambda span, link, far_link: (span >= 3) & link, [("I", [0])], "I")]
    return attend_step(head_span, query_tok, [second], {"I": state}, cases, closed={"I": result})[1]["I"]


def attend_edge(head_span, query_tok, state, second, result):
    cases = [
        (lambda span, link, far_link: (span >= 3) & link, [("E", [0])], ""),
        (lambda span, link, far_link: (span == 2) & link, [("E", [0])], "E"),
    ]
    state, result = attend_step(head_span, query_tok, [second], {"E": state}, cases, closed={"E": result})
    return state["E"], result["E"]


def attend_last(head_span, query_tok, state, third, result):
    cases = [(lambda span, link, far_link: (span >= 3) & link, [("E", [0])], "E")]
    return attend_step(head_span, query_tok, [third], {"E": state}, cases, closed={"E": result})[1]["E"]


def row_edges(role, parts):
    lean = LEAN if role == "E" else 0
    return [0] + [part * FRAME_TOK // parts + lean for part in range(1, parts)] + [FRAME_TOK]


def project(role, attended, part, parts, out_weight, slots, received):
    groups = lax.axis_size("head")
    width = out_weight.shape[1] // groups
    start, stop = row_edges(role, parts)[part : part + 2]
    rows = stop - start

    def kernel(left, right, *rest):
        out = rest[-1]
        group = lax.axis_index("head")
        for index, slot in enumerate(slots):
            column = pl.ds(pl.multiple_of((group ^ slot) * width, width), width)
            sums = jnp.dot(
                left[start:stop, :], right[:, column], preferred_element_type=F32
            )
            for ref, (_, spots) in zip(rest, received):
                sums = sums + ref[:, spots[index] * width : (spots[index] + 1) * width].astype(F32)
            out[:, index * width : (index + 1) * width] = sums.astype(BF16)

    return pl.pallas_call(
        kernel,
        out_shape=jax.ShapeDtypeStruct((rows, len(slots) * width), BF16),
        in_specs=[VMEM] * (2 + len(received)),
        out_specs=VMEM,
        compiler_params=params(),
    )(attended, out_weight, *(array for array, _ in received))


def sum_own(role, attended, parts, out_weight, received):
    groups = lax.axis_size("head")
    width = out_weight.shape[1] // groups
    edges = row_edges(role, parts)
    flat = [(array, spots[0], part) for part in range(parts) for array, spots in received[part]]

    def kernel(left, right, *rest):
        out = rest[-1]
        group = lax.axis_index("head")
        column = pl.ds(pl.multiple_of(group * width, width), width)
        sums = jnp.dot(left[...], right[:, column], preferred_element_type=F32)
        for part in range(parts):
            terms = sums[edges[part] : edges[part + 1]]
            for ref, (_, spot, owner) in zip(rest, flat):
                if owner == part:
                    terms = terms + ref[:, spot * width : (spot + 1) * width].astype(F32)
            out[edges[part] : edges[part + 1], :] = terms

    operands = [attended, out_weight, *(array for array, _, _ in flat)]
    return pl.pallas_call(
        kernel,
        out_shape=jax.ShapeDtypeStruct((FRAME_TOK, width), F32),
        in_specs=[VMEM] * len(operands),
        out_specs=VMEM,
        compiler_params=params(),
    )(*operands)


def finish(role, own, received, frames_here, into):
    parts = len(received)
    edges = row_edges(role, parts)
    width = own.shape[1]

    def kernel(terms, *rest):
        out, buffer, sems = rest[-3:]
        parity = lax.axis_index("frame") % 2
        frame = parity if role == "E" else 1 - parity
        copies = []
        for part in range(parts):
            start, rows = edges[part], edges[part + 1] - edges[part]
            span = slice(start, start + rows)
            buffer[span, :] = (terms[span, :] + rest[part][...].astype(F32)).astype(BF16)
            copies.append(
                pltpu.make_async_copy(
                    buffer.at[pl.ds(start, rows)],
                    out.at[pl.ds(pl.multiple_of(frame * FRAME_TOK + start, 16), rows)],
                    sems.at[part],
                )
            )
            copies[-1].start()
        for copy in copies:
            copy.wait()

    operands = [own, *received]
    in_specs = [VMEM] * len(operands)
    aliases = {}
    if into is not None:
        aliases = {len(operands): 0}
        operands.append(into)
        in_specs.append(HBM)
    return pl.pallas_call(
        kernel,
        out_shape=jax.ShapeDtypeStruct((frames_here * FRAME_TOK, width), BF16),
        in_specs=in_specs,
        out_specs=HBM,
        scratch_shapes=[pltpu.VMEM((FRAME_TOK, width), BF16), pltpu.SemaphoreType.DMA((parts,))],
        input_output_aliases=aliases,
        compiler_params=params(),
    )(*operands)


def body(query_tok, key_tok, value_tok, head_span, out_weight):
    frames = lax.axis_size("frame")
    groups = lax.axis_size("head")
    local_frames = key_tok.shape[0] // FRAME_TOK
    bits = groups.bit_length() - 1
    assert local_frames == 2 and frames % 2 == 0 and groups == 1 << bits and FRAME_TOK % bits == 0

    def swap(value):
        return lax.ppermute(value, "frame", [(i, i ^ 1) for i in range(frames)])

    def across(value):
        pairs = [(i, i + 1) for i in range(1, frames - 1, 2)]
        return lax.ppermute(value, "frame", pairs + [(b, a) for a, b in pairs])

    edge, inner = pack_frames(key_tok, value_tok)
    near = across(edge)
    partner_inner = swap(inner)
    partner_edge = swap(edge)
    second = across(inner)
    third = across(partner_inner)
    state = attend_chip(head_span, query_tok, edge, inner, partner_inner, partner_edge)
    beyond = swap(near)
    state = attend_near(head_span, query_tok, state, near)
    state, attended = attend_beyond(head_span, query_tok, state, beyond)
    attended["I"] = attend_inner(head_span, query_tok, state["I"], second, attended["I"])

    def exchange(value, bit):
        return lax.ppermute(value, "head", [(i, i ^ (1 << bit)) for i in range(groups)])

    held = {role: [list(range(groups)) for _ in range(bits)] for role in "IE"}
    received = {role: [[] for _ in range(bits)] for role in "IE"}

    def gathered(role, part, slots):
        return [(array, [kept.index(s) for s in slots]) for array, kept in received[role][part]]

    def halve(role, stage):
        for part in range(bits):
            bit = (part + stage) % bits
            sent = [s for s in held[role][part] if s >> bit & 1]
            kept = [s for s in held[role][part] if not s >> bit & 1]
            terms = project(role, attended[role], part, bits, out_weight, sent, gathered(role, part, sent))
            received[role][part].append((exchange(terms, bit), kept))
            held[role][part] = kept

    halve("I", 0)
    state_e, attended["E"] = attend_edge(head_span, query_tok, state["E"], second, attended["E"])
    attended["E"] = attend_last(head_span, query_tok, state_e, third, attended["E"])
    for stage in range(bits):
        halve("E", stage)
        if stage + 1 < bits:
            halve("I", stage + 1)
    result = None
    for role in "IE":
        terms = [gathered(role, part, [0]) for part in range(bits)]
        own = sum_own(role, attended[role], bits, out_weight, [t[:-1] for t in terms])
        result = finish(role, own, [t[-1][0] for t in terms], local_frames, result)
    return result


def solution(mesh):
    return jax.shard_map(
        body,
        mesh=mesh,
        in_specs=(
            P("frame", "head"),
            P("frame", "head"),
            P("frame", "head"),
            P("head"),
            P("head", None),
        ),
        out_specs=P("frame", "head"),
        check_vma=False,
    )
```

```python
import jax
import jax.numpy as jnp
from jax import lax
from jax.experimental import pallas as pl
from jax.experimental.pallas import tpu as pltpu
from jax.sharding import PartitionSpec as P


HD = 128
FRAME_TOK = 384
LOG2E = 1.4426950408889634
F32 = jnp.float32
BF16 = jnp.bfloat16
VMEM_LIMIT = 16 << 20
CHUNK = 384
LEAN = 32


def params():
    return pltpu.CompilerParams(vmem_limit_bytes=VMEM_LIMIT)


VMEM = pl.BlockSpec(memory_space=pltpu.VMEM)
SMEM = pl.BlockSpec(memory_space=pltpu.SMEM)
HBM = pl.BlockSpec(memory_space=pltpu.HBM)


def pack_frame(key_tok, value_tok, is_edge):
    def kernel(key, value, out, sems):
        parity = lax.axis_index("frame") % 2
        frame = parity if is_edge else 1 - parity
        copies = [
            pltpu.make_async_copy(
                source.at[pl.ds(pl.multiple_of(frame * FRAME_TOK, FRAME_TOK), FRAME_TOK)],
                out.at[pl.ds(place * FRAME_TOK, FRAME_TOK)],
                sems.at[place],
            )
            for place, source in enumerate((key, value))
        ]
        for copy in copies:
            copy.start()
        for copy in copies:
            copy.wait()

    return pl.pallas_call(
        kernel,
        out_shape=jax.ShapeDtypeStruct((2 * FRAME_TOK, key_tok.shape[1]), BF16),
        in_specs=[HBM, HBM],
        out_specs=VMEM,
        scratch_shapes=[pltpu.SemaphoreType.DMA((2,))],
        compiler_params=params(),
    )(pltpu.with_memory_space_constraint(key_tok, pltpu.HBM), pltpu.with_memory_space_constraint(value_tok, pltpu.HBM))


def attend_step(head_span, query_tok, sources, states, cases, first=False, closed=None):
    heads = query_tok.shape[1] // HD
    frames = lax.axis_size("frame")
    names = list(states)
    closed = closed or {}
    scale = LOG2E / HD**0.5
    keep = first or any(items and not close for _, items, close in cases)

    def kernel(span_ref, query, *refs):
        refs = list(refs)
        chosen = refs.pop()
        loaded = [refs.pop(0) for _ in sources]
        olds = {} if first else {role: [refs.pop(0) for _ in range(3)] for role in names}
        for role in closed:
            if closed[role] is not None:
                refs.pop(0)
        outs = {role: [refs.pop(0) for _ in range(3)] for role in names} if keep else {}
        results = {role: refs.pop(0) for role in closed}
        reads = outs if keep and not first else olds
        seat = lax.axis_index("frame")
        parity = seat % 2
        link = ((parity == 0) & (seat > 0)) | ((parity == 1) & (seat < frames - 1))
        far_link = ((parity == 0) & (seat < frames - 2)) | ((parity == 1) & (seat > 1))
        starts = {"E": parity * FRAME_TOK, "I": (1 - parity) * FRAME_TOK}

        def wide(tops, times):
            return jnp.concatenate([tops] * times, axis=1)

        def take(heads_now, items, close):
            work = []
            for head in heads_now:
                column = pl.ds(pl.multiple_of(head * HD, HD), HD)
                for role, picked in items:
                    keys = jnp.concatenate([loaded[i][:FRAME_TOK, column] for i in picked], axis=0)
                    values = jnp.concatenate([loaded[i][FRAME_TOK:, column] for i in picked], axis=0)
                    values = jnp.concatenate([values, jnp.ones_like(values)], axis=1)
                    for at in range(0, FRAME_TOK, CHUNK):
                        work.append((role, column, slice(at, at + CHUNK), keys, values, len(picked)))
            done = []
            for role, column, rows, keys, values, count in work:
                here = pl.ds(pl.multiple_of(starts[role] + rows.start, CHUNK), CHUNK)
                scores = lax.dot_general(
                    query[here, column], keys, (((1,), (1,)), ((), ())), preferred_element_type=F32
                )
                top = jnp.broadcast_to(jnp.max(scores, axis=1, keepdims=True), (CHUNK, HD))
                fade = None
                if not first:
                    old_top = reads[role][2][rows, column]
                    top = jnp.maximum(top, old_top)
                    fade = jnp.exp2((old_top - top) * scale)
                times = count * FRAME_TOK // HD
                weights = jnp.exp2((scores - wide(top, times)) * scale).astype(BF16)
                mixed = jnp.dot(weights, values, preferred_element_type=F32)
                done.append((role, column, rows, mixed, top, fade))
            for role, column, rows, mixed, top, fade in done:
                acc, total = mixed[:, :HD], mixed[:, HD:]
                if not first:
                    acc = reads[role][0][rows, column] * fade + acc
                    total = reads[role][1][rows, column] * fade + total
                if role in close:
                    results[role][rows, column] = (acc / total).astype(BF16)
                else:
                    outs[role][0][rows, column] = acc
                    outs[role][1][rows, column] = total
                    outs[role][2][rows, column] = top

        def finish_head(head, roles):
            column = pl.ds(pl.multiple_of(head * HD, HD), HD)
            for role in roles:
                acc, total = reads[role][0][:, column], reads[role][1][:, column]
                results[role][:, column] = (acc / total).astype(BF16)

        def collect(condition):
            def add(head, count):
                chosen[count] = head
                return count + condition(span_ref[head], link, far_link).astype(jnp.int32)

            return lax.fori_loop(0, heads, add, jnp.int32(0))

        for condition, items, close in cases:
            count = collect(condition)
            if items:

                def pair(step, carry, items=items, close=close):
                    take((chosen[2 * step], chosen[2 * step + 1]), items, close)
                    return carry

                lax.fori_loop(0, count // 2, pair, 0)
                pl.when(count % 2 == 1)(
                    lambda items=items, close=close, count=count: take((chosen[count - 1],), items, close)
                )
            else:

                def plain(step, carry, close=close):
                    finish_head(chosen[step], close)
                    return carry

                lax.fori_loop(0, count, plain, 0)

    operands = [head_span, query_tok, *sources]
    shapes = []
    aliases = {}
    if not first:
        for index, role in enumerate(names):
            if keep:
                aliases.update({len(operands) + i: 3 * index + i for i in range(3)})
            operands += list(states[role])
    if keep:
        shapes += [jax.ShapeDtypeStruct((FRAME_TOK, heads * HD), F32)] * (3 * len(names))
    for role in closed:
        if closed[role] is not None:
            aliases[len(operands)] = len(shapes)
            operands.append(closed[role])
        shapes.append(jax.ShapeDtypeStruct((FRAME_TOK, heads * HD), BF16))
    out = list(
        pl.pallas_call(
            kernel,
            out_shape=tuple(shapes),
            in_specs=[SMEM] + [VMEM] * (len(operands) - 1),
            out_specs=(VMEM,) * len(shapes),
            scratch_shapes=[pltpu.SMEM((heads + 1,), jnp.int32)],
            input_output_aliases=aliases,
            compiler_params=params(),
        )(*operands)
    )
    new_states = {role: [out.pop(0) for _ in range(3)] for role in names} if keep else {}
    return new_states, {role: out.pop(0) for role in closed}


def attend_chip(head_span, query_tok, edge, inner, partner_inner, partner_edge):
    order = {"E": [0, 1, 2, 3], "I": [1, 0, 2, 3]}
    reach = {"E": [1, 2, 3, 4], "I": [1, 3, 4, 4]}
    cases = [
        (
            lambda span, link, far_link, limit=limit: span == limit,
            [(role, order[role][: reach[role][limit]]) for role in "EI"],
            "",
        )
        for limit in range(4)
    ]
    return attend_step(
        head_span, query_tok, [edge, inner, partner_inner, partner_edge], {"E": None, "I": None}, cases, first=True
    )[0]


def attend_near(head_span, query_tok, state, near):
    cases = [
        (lambda span, link, far_link: (span >= 2) & link, [("E", [0]), ("I", [0])], ""),
        (lambda span, link, far_link: (span == 1) & link, [("E", [0])], ""),
    ]
    return attend_step(head_span, query_tok, [near], state, cases)[0]


def attend_beyond(head_span, query_tok, state, beyond):
    cases = [
        (lambda span, link, far_link: (span >= 3) & far_link, [("I", [0])], ""),
        (lambda span, link, far_link: (span < 3) | jnp.logical_not(link), [], "I"),
        (lambda span, link, far_link: (span < 2) | jnp.logical_not(link), [], "E"),
    ]
    return attend_step(head_span, query_tok, [beyond], state, cases, closed={"I": None, "E": None})


def attend_inner(head_span, query_tok, state, second, result):
    cases = [(lambda span, link, far_link: (span >= 3) & link, [("I", [0])], "I")]
    return attend_step(head_span, query_tok, [second], {"I": state}, cases, closed={"I": result})[1]["I"]


def attend_edge(head_span, query_tok, state, second, result):
    cases = [
        (lambda span, link, far_link: (span >= 3) & link, [("E", [0])], ""),
        (lambda span, link, far_link: (span == 2) & link, [("E", [0])], "E"),
    ]
    state, result = attend_step(head_span, query_tok, [second], {"E": state}, cases, closed={"E": result})
    return state["E"], result["E"]


def attend_last(head_span, query_tok, state, third, result):
    cases = [(lambda span, link, far_link: (span >= 3) & link, [("E", [0])], "E")]
    return attend_step(head_span, query_tok, [third], {"E": state}, cases, closed={"E": result})[1]["E"]


def row_edges(role, parts):
    lean = LEAN if role == "E" else 0
    return [0] + [part * FRAME_TOK // parts + lean for part in range(1, parts)] + [FRAME_TOK]


def project(role, attended, part, parts, out_weight, slots, received):
    groups = lax.axis_size("head")
    width = out_weight.shape[1] // groups
    start, stop = row_edges(role, parts)[part : part + 2]
    rows = stop - start

    def kernel(left, right, *rest):
        out = rest[-1]
        group = lax.axis_index("head")
        for index, slot in enumerate(slots):
            column = pl.ds(pl.multiple_of((group ^ slot) * width, width), width)
            sums = jnp.dot(
                left[start:stop, :], right[:, column], preferred_element_type=F32
            )
            for ref, (_, spots) in zip(rest, received):
                sums = sums + ref[:, spots[index] * width : (spots[index] + 1) * width].astype(F32)
            out[:, index * width : (index + 1) * width] = sums.astype(BF16)

    return pl.pallas_call(
        kernel,
        out_shape=jax.ShapeDtypeStruct((rows, len(slots) * width), BF16),
        in_specs=[VMEM] * (2 + len(received)),
        out_specs=VMEM,
        compiler_params=params(),
    )(attended, out_weight, *(array for array, _ in received))


def sum_own(role, attended, parts, out_weight, received):
    groups = lax.axis_size("head")
    width = out_weight.shape[1] // groups
    edges = row_edges(role, parts)
    flat = [(array, spots[0], part) for part in range(parts) for array, spots in received[part]]

    def kernel(left, right, *rest):
        out = rest[-1]
        group = lax.axis_index("head")
        column = pl.ds(pl.multiple_of(group * width, width), width)
        sums = jnp.dot(left[...], right[:, column], preferred_element_type=F32)
        for part in range(parts):
            terms = sums[edges[part] : edges[part + 1]]
            for ref, (_, spot, owner) in zip(rest, flat):
                if owner == part:
                    terms = terms + ref[:, spot * width : (spot + 1) * width].astype(F32)
            out[edges[part] : edges[part + 1], :] = terms

    operands = [attended, out_weight, *(array for array, _, _ in flat)]
    return pl.pallas_call(
        kernel,
        out_shape=jax.ShapeDtypeStruct((FRAME_TOK, width), F32),
        in_specs=[VMEM] * len(operands),
        out_specs=VMEM,
        compiler_params=params(),
    )(*operands)


def finish(role, own, received, part, parts, frames_here, into):
    start, stop = row_edges(role, parts)[part : part + 2]
    rows = stop - start
    width = own.shape[1]

    def kernel(terms, last, *rest):
        out, buffer, sem = rest[-3:]
        parity = lax.axis_index("frame") % 2
        frame = parity if role == "E" else 1 - parity
        buffer[...] = (terms[start:stop, :] + last[...].astype(F32)).astype(BF16)
        copy = pltpu.make_async_copy(
            buffer, out.at[pl.ds(pl.multiple_of(frame * FRAME_TOK + start, 16), rows)], sem
        )
        copy.start()
        copy.wait()

    operands = [own, received]
    in_specs = [VMEM] * len(operands)
    aliases = {}
    if into is not None:
        aliases = {len(operands): 0}
        operands.append(into)
        in_specs.append(HBM)
    return pl.pallas_call(
        kernel,
        out_shape=jax.ShapeDtypeStruct((frames_here * FRAME_TOK, width), BF16),
        in_specs=in_specs,
        out_specs=HBM,
        scratch_shapes=[pltpu.VMEM((rows, width), BF16), pltpu.SemaphoreType.DMA(())],
        input_output_aliases=aliases,
        compiler_params=params(),
    )(*operands)


def body(query_tok, key_tok, value_tok, head_span, out_weight):
    frames = lax.axis_size("frame")
    groups = lax.axis_size("head")
    local_frames = key_tok.shape[0] // FRAME_TOK
    bits = groups.bit_length() - 1
    assert local_frames == 2 and frames % 2 == 0 and groups == 1 << bits and FRAME_TOK % bits == 0

    def swap(value):
        return lax.ppermute(value, "frame", [(i, i ^ 1) for i in range(frames)])

    def across(value):
        pairs = [(i, i + 1) for i in range(1, frames - 1, 2)]
        return lax.ppermute(value, "frame", pairs + [(b, a) for a, b in pairs])

    edge = pack_frame(key_tok, value_tok, True)
    inner = pack_frame(key_tok, value_tok, False)
    near = across(edge)
    partner_inner = swap(inner)
    partner_edge = swap(edge)
    second = across(inner)
    third = across(partner_inner)
    state = attend_chip(head_span, query_tok, edge, inner, partner_inner, partner_edge)
    beyond = swap(near)
    state = attend_near(head_span, query_tok, state, near)
    state, attended = attend_beyond(head_span, query_tok, state, beyond)
    attended["I"] = attend_inner(head_span, query_tok, state["I"], second, attended["I"])

    def exchange(value, bit):
        return lax.ppermute(value, "head", [(i, i ^ (1 << bit)) for i in range(groups)])

    held = {role: [list(range(groups)) for _ in range(bits)] for role in "IE"}
    received = {role: [[] for _ in range(bits)] for role in "IE"}

    def gathered(role, part, slots):
        return [(array, [kept.index(s) for s in slots]) for array, kept in received[role][part]]

    def halve(role, stage):
        for part in range(bits):
            bit = (part + stage) % bits
            sent = [s for s in held[role][part] if s >> bit & 1]
            kept = [s for s in held[role][part] if not s >> bit & 1]
            terms = project(role, attended[role], part, bits, out_weight, sent, gathered(role, part, sent))
            received[role][part].append((exchange(terms, bit), kept))
            held[role][part] = kept

    halve("I", 0)
    state_e, attended["E"] = attend_edge(head_span, query_tok, state["E"], second, attended["E"])
    attended["E"] = attend_last(head_span, query_tok, state_e, third, attended["E"])
    for stage in range(bits):
        halve("E", stage)
        if stage + 1 < bits:
            halve("I", stage + 1)
    result = None
    for role in "IE":
        terms = [gathered(role, part, [0]) for part in range(bits)]
        own = sum_own(role, attended[role], bits, out_weight, [t[:-1] for t in terms])
        for part in reversed(range(bits)):
            result = finish(role, own, terms[part][-1][0], part, bits, local_frames, result)
    return result


def solution(mesh):
    return jax.shard_map(
        body,
        mesh=mesh,
        in_specs=(
            P("frame", "head"),
            P("frame", "head"),
            P("frame", "head"),
            P("head"),
            P("head", None),
        ),
        out_specs=P("frame", "head"),
        check_vma=False,
    )
```

```python
import jax
import jax.numpy as jnp
from jax import lax
from jax.experimental import pallas as pl
from jax.experimental.pallas import tpu as pltpu
from jax.sharding import PartitionSpec as P


HD = 128
FRAME_TOK = 384
LOG2E = 1.4426950408889634
F32 = jnp.float32
BF16 = jnp.bfloat16
VMEM_LIMIT = 16 << 20
CHUNK = 384


def params():
    return pltpu.CompilerParams(vmem_limit_bytes=VMEM_LIMIT)


VMEM = pl.BlockSpec(memory_space=pltpu.VMEM)
SMEM = pl.BlockSpec(memory_space=pltpu.SMEM)
HBM = pl.BlockSpec(memory_space=pltpu.HBM)


def pack_frames(key_tok, value_tok):
    parity = lax.axis_index("frame") % 2

    def packed(key, value, frame):
        rows = [lax.dynamic_slice_in_dim(array, frame * FRAME_TOK, FRAME_TOK, 0) for array in (key, value)]
        return jnp.concatenate(rows, axis=0)

    edge = packed(key_tok, value_tok, parity)
    edge, key_tok, value_tok = lax.optimization_barrier((edge, key_tok, value_tok))
    return edge, packed(key_tok, value_tok, 1 - parity)


def attend_step(head_span, query_tok, sources, states, cases, first=False, closed=None):
    heads = query_tok.shape[1] // HD
    frames = lax.axis_size("frame")
    names = list(states)
    closed = closed or {}
    scale = LOG2E / HD**0.5
    keep = first or any(items and not close for _, items, close in cases)

    def kernel(span_ref, query, *refs):
        refs = list(refs)
        chosen = refs.pop()
        loaded = [refs.pop(0) for _ in sources]
        olds = {} if first else {role: [refs.pop(0) for _ in range(3)] for role in names}
        for role in closed:
            if closed[role] is not None:
                refs.pop(0)
        outs = {role: [refs.pop(0) for _ in range(3)] for role in names} if keep else {}
        results = {role: refs.pop(0) for role in closed}
        reads = outs if keep and not first else olds
        seat = lax.axis_index("frame")
        parity = seat % 2
        link = ((parity == 0) & (seat > 0)) | ((parity == 1) & (seat < frames - 1))
        far_link = ((parity == 0) & (seat < frames - 2)) | ((parity == 1) & (seat > 1))
        starts = {"E": parity * FRAME_TOK, "I": (1 - parity) * FRAME_TOK}

        def wide(tops, times):
            return jnp.concatenate([tops] * times, axis=1)

        def take(heads_now, items, close):
            work = []
            for head in heads_now:
                column = pl.ds(pl.multiple_of(head * HD, HD), HD)
                for role, picked in items:
                    keys = jnp.concatenate([loaded[i][:FRAME_TOK, column] for i in picked], axis=0)
                    values = jnp.concatenate([loaded[i][FRAME_TOK:, column] for i in picked], axis=0)
                    values = jnp.concatenate([values, jnp.ones_like(values)], axis=1)
                    for at in range(0, FRAME_TOK, CHUNK):
                        work.append((role, column, slice(at, at + CHUNK), keys, values, len(picked)))
            done = []
            for role, column, rows, keys, values, count in work:
                here = pl.ds(pl.multiple_of(starts[role] + rows.start, CHUNK), CHUNK)
                scores = lax.dot_general(
                    query[here, column], keys, (((1,), (1,)), ((), ())), preferred_element_type=F32
                )
                top = jnp.broadcast_to(jnp.max(scores, axis=1, keepdims=True), (CHUNK, HD))
                fade = None
                if not first:
                    old_top = reads[role][2][rows, column]
                    top = jnp.maximum(top, old_top)
                    fade = jnp.exp2((old_top - top) * scale)
                times = count * FRAME_TOK // HD
                weights = jnp.exp2((scores - wide(top, times)) * scale).astype(BF16)
                mixed = jnp.dot(weights, values, preferred_element_type=F32)
                done.append((role, column, rows, mixed, top, fade))
            for role, column, rows, mixed, top, fade in done:
                acc, total = mixed[:, :HD], mixed[:, HD:]
                if not first:
                    acc = reads[role][0][rows, column] * fade + acc
                    total = reads[role][1][rows, column] * fade + total
                if role in close:
                    results[role][rows, column] = (acc / total).astype(BF16)
                else:
                    outs[role][0][rows, column] = acc
                    outs[role][1][rows, column] = total
                    outs[role][2][rows, column] = top

        def finish_head(head, roles):
            column = pl.ds(pl.multiple_of(head * HD, HD), HD)
            for role in roles:
                acc, total = reads[role][0][:, column], reads[role][1][:, column]
                results[role][:, column] = (acc / total).astype(BF16)

        def collect(condition):
            def add(head, count):
                chosen[count] = head
                return count + condition(span_ref[head], link, far_link).astype(jnp.int32)

            return lax.fori_loop(0, heads, add, jnp.int32(0))

        for condition, items, close in cases:
            count = collect(condition)
            if items:

                def pair(step, carry, items=items, close=close):
                    take((chosen[2 * step], chosen[2 * step + 1]), items, close)
                    return carry

                lax.fori_loop(0, count // 2, pair, 0)
                pl.when(count % 2 == 1)(
                    lambda items=items, close=close, count=count: take((chosen[jnp.maximum(count - 1, 0)],), items, close)
                )
            else:

                def plain(step, carry, close=close):
                    finish_head(chosen[step], close)
                    return carry

                lax.fori_loop(0, count, plain, 0)

    operands = [head_span, query_tok, *sources]
    shapes = []
    aliases = {}
    if not first:
        for index, role in enumerate(names):
            if keep:
                aliases.update({len(operands) + i: 3 * index + i for i in range(3)})
            operands += list(states[role])
    if keep:
        shapes += [jax.ShapeDtypeStruct((FRAME_TOK, heads * HD), F32)] * (3 * len(names))
    for role in closed:
        if closed[role] is not None:
            aliases[len(operands)] = len(shapes)
            operands.append(closed[role])
        shapes.append(jax.ShapeDtypeStruct((FRAME_TOK, heads * HD), BF16))
    out = list(
        pl.pallas_call(
            kernel,
            out_shape=tuple(shapes),
            in_specs=[SMEM] + [VMEM] * (len(operands) - 1),
            out_specs=(VMEM,) * len(shapes),
            scratch_shapes=[pltpu.SMEM((heads + 1,), jnp.int32)],
            input_output_aliases=aliases,
            compiler_params=params(),
        )(*operands)
    )
    new_states = {role: [out.pop(0) for _ in range(3)] for role in names} if keep else {}
    return new_states, {role: out.pop(0) for role in closed}


def attend_chip(head_span, query_tok, edge, inner, partner_inner, partner_edge):
    order = {"E": [0, 1, 2, 3], "I": [1, 0, 2, 3]}
    reach = {"E": [1, 2, 3, 4], "I": [1, 3, 4, 4]}
    cases = [
        (
            lambda span, link, far_link, limit=limit: span == limit,
            [(role, order[role][: reach[role][limit]]) for role in "EI"],
            "",
        )
        for limit in range(4)
    ]
    return attend_step(
        head_span, query_tok, [edge, inner, partner_inner, partner_edge], {"E": None, "I": None}, cases, first=True
    )[0]


def attend_near(head_span, query_tok, state, near):
    cases = [
        (lambda span, link, far_link: (span >= 2) & link, [("E", [0]), ("I", [0])], ""),
        (lambda span, link, far_link: (span == 1) & link, [("E", [0])], ""),
    ]
    return attend_step(head_span, query_tok, [near], state, cases)[0]


def attend_beyond(head_span, query_tok, state, beyond):
    cases = [
        (lambda span, link, far_link: (span >= 3) & far_link, [("I", [0])], ""),
        (lambda span, link, far_link: (span < 3) | jnp.logical_not(link), [], "I"),
        (lambda span, link, far_link: (span < 2) | jnp.logical_not(link), [], "E"),
    ]
    return attend_step(head_span, query_tok, [beyond], state, cases, closed={"I": None, "E": None})


def attend_inner(head_span, query_tok, state, second, result):
    cases = [(lambda span, link, far_link: (span >= 3) & link, [("I", [0])], "I")]
    return attend_step(head_span, query_tok, [second], {"I": state}, cases, closed={"I": result})[1]["I"]


def attend_edge(head_span, query_tok, state, second, result):
    cases = [
        (lambda span, link, far_link: (span >= 3) & link, [("E", [0])], ""),
        (lambda span, link, far_link: (span == 2) & link, [("E", [0])], "E"),
    ]
    state, result = attend_step(head_span, query_tok, [second], {"E": state}, cases, closed={"E": result})
    return state["E"], result["E"]


def attend_last(head_span, query_tok, state, third, result):
    cases = [(lambda span, link, far_link: (span >= 3) & link, [("E", [0])], "E")]
    return attend_step(head_span, query_tok, [third], {"E": state}, cases, closed={"E": result})[1]["E"]


def row_edges(parts):
    return [part * FRAME_TOK // parts for part in range(parts + 1)]


def mesh_bit(stage, part, core, bits):
    return (stage + part + core) % bits


def owner_of(slot, part, core, bits):
    return sum(1 << mesh_bit(stage, part, core, bits) for stage in range(bits) if slot >> stage & 1)


def project(attended, part, parts, out_weight, slots, received):
    groups = lax.axis_size("head")
    width = out_weight.shape[1] // groups
    start, stop = row_edges(parts)[part : part + 2]
    rows = stop - start

    def kernel(left, right, *rest):
        out = rest[-1]
        group = lax.axis_index("head")
        core = lax.axis_index("frame") % 2
        for index, slot in enumerate(slots):
            toward = jnp.where(
                core == 0, owner_of(slot, part, 0, parts), owner_of(slot, part, 1, parts)
            )
            column = pl.ds(pl.multiple_of((group ^ toward) * width, width), width)
            sums = jnp.dot(
                left[start:stop, :], right[:, column], preferred_element_type=F32
            )
            for ref, (_, spots) in zip(rest, received):
                sums = sums + ref[:, spots[index] * width : (spots[index] + 1) * width].astype(F32)
            out[:, index * width : (index + 1) * width] = sums.astype(BF16)

    return pl.pallas_call(
        kernel,
        out_shape=jax.ShapeDtypeStruct((rows, len(slots) * width), BF16),
        in_specs=[VMEM] * (2 + len(received)),
        out_specs=VMEM,
        compiler_params=params(),
    )(attended, out_weight, *(array for array, _ in received))


def sum_own(attended, parts, out_weight, received):
    groups = lax.axis_size("head")
    width = out_weight.shape[1] // groups
    edges = row_edges(parts)
    flat = [(array, spots[0], part) for part in range(parts) for array, spots in received[part]]

    def kernel(left, right, *rest):
        out = rest[-1]
        group = lax.axis_index("head")
        column = pl.ds(pl.multiple_of(group * width, width), width)
        sums = jnp.dot(left[...], right[:, column], preferred_element_type=F32)
        for part in range(parts):
            terms = sums[edges[part] : edges[part + 1]]
            for ref, (_, spot, owner) in zip(rest, flat):
                if owner == part:
                    terms = terms + ref[:, spot * width : (spot + 1) * width].astype(F32)
            out[edges[part] : edges[part + 1], :] = terms

    operands = [attended, out_weight, *(array for array, _, _ in flat)]
    return pl.pallas_call(
        kernel,
        out_shape=jax.ShapeDtypeStruct((FRAME_TOK, width), F32),
        in_specs=[VMEM] * len(operands),
        out_specs=VMEM,
        compiler_params=params(),
    )(*operands)


def finish(role, own, received, frames_here, into):
    parts = len(received)
    edges = row_edges(parts)
    width = own.shape[1]

    def kernel(terms, *rest):
        out, buffer, sems = rest[-3:]
        parity = lax.axis_index("frame") % 2
        frame = parity if role == "E" else 1 - parity
        copies = []
        for part in range(parts):
            start, rows = edges[part], edges[part + 1] - edges[part]
            span = slice(start, start + rows)
            buffer[span, :] = (terms[span, :] + rest[part][...].astype(F32)).astype(BF16)
            copies.append(
                pltpu.make_async_copy(
                    buffer.at[pl.ds(start, rows)],
                    out.at[pl.ds(pl.multiple_of(frame * FRAME_TOK + start, 16), rows)],
                    sems.at[part],
                )
            )
            copies[-1].start()
        for copy in copies:
            copy.wait()

    operands = [own, *received]
    in_specs = [VMEM] * len(operands)
    aliases = {}
    if into is not None:
        aliases = {len(operands): 0}
        operands.append(into)
        in_specs.append(HBM)
    return pl.pallas_call(
        kernel,
        out_shape=jax.ShapeDtypeStruct((frames_here * FRAME_TOK, width), BF16),
        in_specs=in_specs,
        out_specs=HBM,
        scratch_shapes=[pltpu.VMEM((FRAME_TOK, width), BF16), pltpu.SemaphoreType.DMA((parts,))],
        input_output_aliases=aliases,
        compiler_params=params(),
    )(*operands)


def body(query_tok, key_tok, value_tok, head_span, out_weight):
    frames = lax.axis_size("frame")
    groups = lax.axis_size("head")
    local_frames = key_tok.shape[0] // FRAME_TOK
    bits = groups.bit_length() - 1
    assert local_frames == 2 and frames % 2 == 0 and groups == 1 << bits and FRAME_TOK % bits == 0

    def swap(value):
        return lax.ppermute(value, "frame", [(i, i ^ 1) for i in range(frames)])

    def across(value):
        pairs = [(i, i + 1) for i in range(1, frames - 1, 2)]
        return lax.ppermute(value, "frame", pairs + [(b, a) for a, b in pairs])

    edge, inner = pack_frames(key_tok, value_tok)
    near = across(edge)
    partner_inner = swap(inner)
    partner_edge = swap(edge)
    second = across(inner)
    third = across(partner_inner)
    state = attend_chip(head_span, query_tok, edge, inner, partner_inner, partner_edge)
    beyond = swap(near)
    state = attend_near(head_span, query_tok, state, near)
    state, attended = attend_beyond(head_span, query_tok, state, beyond)
    attended["I"] = attend_inner(head_span, query_tok, state["I"], second, attended["I"])

    def exchange(value, stage, part):
        pairs = []
        for head in range(groups):
            for place in range(frames):
                other = head ^ (1 << mesh_bit(stage, part, place % 2, bits))
                pairs.append((head * frames + place, other * frames + place))
        return lax.ppermute(value, ("head", "frame"), pairs)

    held = {role: [list(range(groups)) for _ in range(bits)] for role in "IE"}
    received = {role: [[] for _ in range(bits)] for role in "IE"}

    def gathered(role, part, slots):
        return [(array, [kept.index(s) for s in slots]) for array, kept in received[role][part]]

    def halve(role, stage):
        for part in range(bits):
            sent = [s for s in held[role][part] if s >> stage & 1]
            kept = [s for s in held[role][part] if not s >> stage & 1]
            terms = project(attended[role], part, bits, out_weight, sent, gathered(role, part, sent))
            received[role][part].append((exchange(terms, stage, part), kept))
            held[role][part] = kept

    halve("I", 0)
    state_e, attended["E"] = attend_edge(head_span, query_tok, state["E"], second, attended["E"])
    attended["E"] = attend_last(head_span, query_tok, state_e, third, attended["E"])
    for stage in range(bits):
        halve("E", stage)
        if stage + 1 < bits:
            halve("I", stage + 1)
    result = None
    for role in "IE":
        terms = [gathered(role, part, [0]) for part in range(bits)]
        own = sum_own(attended[role], bits, out_weight, [t[:-1] for t in terms])
        result = finish(role, own, [t[-1][0] for t in terms], local_frames, result)
    return result


def solution(mesh):
    return jax.shard_map(
        body,
        mesh=mesh,
        in_specs=(
            P("frame", "head"),
            P("frame", "head"),
            P("frame", "head"),
            P("head"),
            P("head", None),
        ),
        out_specs=P("frame", "head"),
        check_vma=False,
    )
```

```python
import jax
import jax.numpy as jnp
from jax import lax
from jax.experimental import pallas as pl
from jax.experimental.pallas import tpu as pltpu
from jax.sharding import PartitionSpec as P


HD = 128
FRAME_TOK = 384
LOG2E = 1.4426950408889634
F32 = jnp.float32
BF16 = jnp.bfloat16
VMEM_LIMIT = 16 << 20
CHUNK = 384


def params():
    return pltpu.CompilerParams(vmem_limit_bytes=VMEM_LIMIT)


VMEM = pl.BlockSpec(memory_space=pltpu.VMEM)
SMEM = pl.BlockSpec(memory_space=pltpu.SMEM)
HBM = pl.BlockSpec(memory_space=pltpu.HBM)


def pack_frame(key_tok, value_tok, is_edge):
    def kernel(key, value, out, sems):
        parity = lax.axis_index("frame") % 2
        frame = parity if is_edge else 1 - parity
        copies = [
            pltpu.make_async_copy(
                source.at[pl.ds(pl.multiple_of(frame * FRAME_TOK, FRAME_TOK), FRAME_TOK)],
                out.at[pl.ds(place * FRAME_TOK, FRAME_TOK)],
                sems.at[place],
            )
            for place, source in enumerate((key, value))
        ]
        for copy in copies:
            copy.start()
        for copy in copies:
            copy.wait()

    return pl.pallas_call(
        kernel,
        out_shape=jax.ShapeDtypeStruct((2 * FRAME_TOK, key_tok.shape[1]), BF16),
        in_specs=[HBM, HBM],
        out_specs=VMEM,
        scratch_shapes=[pltpu.SemaphoreType.DMA((2,))],
        compiler_params=params(),
    )(pltpu.with_memory_space_constraint(key_tok, pltpu.HBM), pltpu.with_memory_space_constraint(value_tok, pltpu.HBM))


def attend_step(head_span, query_tok, sources, states, cases, first=False, closed=None):
    heads = query_tok.shape[1] // HD
    frames = lax.axis_size("frame")
    names = list(states)
    closed = closed or {}
    scale = LOG2E / HD**0.5
    keep = first or any(items and not close for _, items, close in cases)

    def kernel(span_ref, query, *refs):
        refs = list(refs)
        chosen = refs.pop()
        loaded = [refs.pop(0) for _ in sources]
        olds = {} if first else {role: [refs.pop(0) for _ in range(3)] for role in names}
        for role in closed:
            if closed[role] is not None:
                refs.pop(0)
        outs = {role: [refs.pop(0) for _ in range(3)] for role in names} if keep else {}
        results = {role: refs.pop(0) for role in closed}
        reads = outs if keep and not first else olds
        seat = lax.axis_index("frame")
        parity = seat % 2
        link = ((parity == 0) & (seat > 0)) | ((parity == 1) & (seat < frames - 1))
        far_link = ((parity == 0) & (seat < frames - 2)) | ((parity == 1) & (seat > 1))
        starts = {"E": parity * FRAME_TOK, "I": (1 - parity) * FRAME_TOK}

        def wide(tops, times):
            return jnp.concatenate([tops] * times, axis=1)

        def take(heads_now, items, close):
            work = []
            for head in heads_now:
                column = pl.ds(pl.multiple_of(head * HD, HD), HD)
                for role, picked in items:
                    keys = jnp.concatenate([loaded[i][:FRAME_TOK, column] for i in picked], axis=0)
                    values = jnp.concatenate([loaded[i][FRAME_TOK:, column] for i in picked], axis=0)
                    values = jnp.concatenate([values, jnp.ones_like(values)], axis=1)
                    for at in range(0, FRAME_TOK, CHUNK):
                        work.append((role, column, slice(at, at + CHUNK), keys, values, len(picked)))
            done = []
            for role, column, rows, keys, values, count in work:
                here = pl.ds(pl.multiple_of(starts[role] + rows.start, CHUNK), CHUNK)
                scores = lax.dot_general(
                    query[here, column], keys, (((1,), (1,)), ((), ())), preferred_element_type=F32
                )
                top = jnp.broadcast_to(jnp.max(scores, axis=1, keepdims=True), (CHUNK, HD))
                fade = None
                if not first:
                    old_top = reads[role][2][rows, column]
                    top = jnp.maximum(top, old_top)
                    fade = jnp.exp2((old_top - top) * scale)
                times = count * FRAME_TOK // HD
                weights = jnp.exp2((scores - wide(top, times)) * scale).astype(BF16)
                mixed = jnp.dot(weights, values, preferred_element_type=F32)
                done.append((role, column, rows, mixed, top, fade))
            for role, column, rows, mixed, top, fade in done:
                acc, total = mixed[:, :HD], mixed[:, HD:]
                if not first:
                    acc = reads[role][0][rows, column] * fade + acc
                    total = reads[role][1][rows, column] * fade + total
                if role in close:
                    results[role][rows, column] = (acc / total).astype(BF16)
                else:
                    outs[role][0][rows, column] = acc
                    outs[role][1][rows, column] = total
                    outs[role][2][rows, column] = top

        def finish_head(head, roles):
            column = pl.ds(pl.multiple_of(head * HD, HD), HD)
            for role in roles:
                acc, total = reads[role][0][:, column], reads[role][1][:, column]
                results[role][:, column] = (acc / total).astype(BF16)

        def collect(condition):
            def add(head, count):
                chosen[count] = head
                return count + condition(span_ref[head], link, far_link).astype(jnp.int32)

            return lax.fori_loop(0, heads, add, jnp.int32(0))

        for condition, items, close in cases:
            count = collect(condition)
            if items:

                def pair(step, carry, items=items, close=close):
                    take((chosen[2 * step], chosen[2 * step + 1]), items, close)
                    return carry

                lax.fori_loop(0, count // 2, pair, 0)
                pl.when(count % 2 == 1)(
                    lambda items=items, close=close, count=count: take((chosen[jnp.maximum(count - 1, 0)],), items, close)
                )
            else:

                def plain(step, carry, close=close):
                    finish_head(chosen[step], close)
                    return carry

                lax.fori_loop(0, count, plain, 0)

    operands = [head_span, query_tok, *sources]
    shapes = []
    aliases = {}
    if not first:
        for index, role in enumerate(names):
            if keep:
                aliases.update({len(operands) + i: 3 * index + i for i in range(3)})
            operands += list(states[role])
    if keep:
        shapes += [jax.ShapeDtypeStruct((FRAME_TOK, heads * HD), F32)] * (3 * len(names))
    for role in closed:
        if closed[role] is not None:
            aliases[len(operands)] = len(shapes)
            operands.append(closed[role])
        shapes.append(jax.ShapeDtypeStruct((FRAME_TOK, heads * HD), BF16))
    out = list(
        pl.pallas_call(
            kernel,
            out_shape=tuple(shapes),
            in_specs=[SMEM] + [VMEM] * (len(operands) - 1),
            out_specs=(VMEM,) * len(shapes),
            scratch_shapes=[pltpu.SMEM((heads + 1,), jnp.int32)],
            input_output_aliases=aliases,
            compiler_params=params(),
        )(*operands)
    )
    new_states = {role: [out.pop(0) for _ in range(3)] for role in names} if keep else {}
    return new_states, {role: out.pop(0) for role in closed}


def attend_chip(head_span, query_tok, edge, inner, partner_inner, partner_edge):
    order = {"E": [0, 1, 2, 3], "I": [1, 0, 2, 3]}
    reach = {"E": [1, 2, 3, 4], "I": [1, 3, 4, 4]}
    cases = [
        (
            lambda span, link, far_link, limit=limit: span == limit,
            [(role, order[role][: reach[role][limit]]) for role in "EI"],
            "",
        )
        for limit in range(4)
    ]
    return attend_step(
        head_span, query_tok, [edge, inner, partner_inner, partner_edge], {"E": None, "I": None}, cases, first=True
    )[0]


def attend_near(head_span, query_tok, state, near):
    cases = [
        (lambda span, link, far_link: (span >= 2) & link, [("E", [0]), ("I", [0])], ""),
        (lambda span, link, far_link: (span == 1) & link, [("E", [0])], ""),
    ]
    return attend_step(head_span, query_tok, [near], state, cases)[0]


def attend_beyond(head_span, query_tok, state, beyond):
    cases = [
        (lambda span, link, far_link: (span >= 3) & far_link, [("I", [0])], ""),
        (lambda span, link, far_link: (span < 3) | jnp.logical_not(link), [], "I"),
        (lambda span, link, far_link: (span < 2) | jnp.logical_not(link), [], "E"),
    ]
    return attend_step(head_span, query_tok, [beyond], state, cases, closed={"I": None, "E": None})


def attend_inner(head_span, query_tok, state, second, result):
    cases = [(lambda span, link, far_link: (span >= 3) & link, [("I", [0])], "I")]
    return attend_step(head_span, query_tok, [second], {"I": state}, cases, closed={"I": result})[1]["I"]


def attend_edge(head_span, query_tok, state, second, result):
    cases = [
        (lambda span, link, far_link: (span >= 3) & link, [("E", [0])], ""),
        (lambda span, link, far_link: (span == 2) & link, [("E", [0])], "E"),
    ]
    state, result = attend_step(head_span, query_tok, [second], {"E": state}, cases, closed={"E": result})
    return state["E"], result["E"]


def attend_last(head_span, query_tok, state, third, result):
    cases = [(lambda span, link, far_link: (span >= 3) & link, [("E", [0])], "E")]
    return attend_step(head_span, query_tok, [third], {"E": state}, cases, closed={"E": result})[1]["E"]


def row_edges(parts):
    return [part * FRAME_TOK // parts for part in range(parts + 1)]


def mesh_bit(stage, part, core, bits):
    return (stage + part + core) % bits


def owner_of(slot, part, core, bits):
    return sum(1 << mesh_bit(stage, part, core, bits) for stage in range(bits) if slot >> stage & 1)


def project(attended, part, parts, out_weight, slots, received):
    groups = lax.axis_size("head")
    width = out_weight.shape[1] // groups
    start, stop = row_edges(parts)[part : part + 2]
    rows = stop - start

    def kernel(left, right, *rest):
        out = rest[-1]
        group = lax.axis_index("head")
        core = lax.axis_index("frame") % 2
        for index, slot in enumerate(slots):
            toward = jnp.where(
                core == 0, owner_of(slot, part, 0, parts), owner_of(slot, part, 1, parts)
            )
            column = pl.ds(pl.multiple_of((group ^ toward) * width, width), width)
            sums = jnp.dot(
                left[start:stop, :], right[:, column], preferred_element_type=F32
            )
            for ref, (_, spots) in zip(rest, received):
                sums = sums + ref[:, spots[index] * width : (spots[index] + 1) * width].astype(F32)
            out[:, index * width : (index + 1) * width] = sums.astype(BF16)

    return pl.pallas_call(
        kernel,
        out_shape=jax.ShapeDtypeStruct((rows, len(slots) * width), BF16),
        in_specs=[VMEM] * (2 + len(received)),
        out_specs=VMEM,
        compiler_params=params(),
    )(attended, out_weight, *(array for array, _ in received))


def sum_own(attended, parts, out_weight, received):
    groups = lax.axis_size("head")
    width = out_weight.shape[1] // groups
    edges = row_edges(parts)
    flat = [(array, spots[0], part) for part in range(parts) for array, spots in received[part]]

    def kernel(left, right, *rest):
        out = rest[-1]
        group = lax.axis_index("head")
        column = pl.ds(pl.multiple_of(group * width, width), width)
        sums = jnp.dot(left[...], right[:, column], preferred_element_type=F32)
        for part in range(parts):
            terms = sums[edges[part] : edges[part + 1]]
            for ref, (_, spot, owner) in zip(rest, flat):
                if owner == part:
                    terms = terms + ref[:, spot * width : (spot + 1) * width].astype(F32)
            out[edges[part] : edges[part + 1], :] = terms

    operands = [attended, out_weight, *(array for array, _, _ in flat)]
    return pl.pallas_call(
        kernel,
        out_shape=jax.ShapeDtypeStruct((FRAME_TOK, width), F32),
        in_specs=[VMEM] * len(operands),
        out_specs=VMEM,
        compiler_params=params(),
    )(*operands)


def finish(role, own, received, frames_here, into):
    parts = len(received)
    edges = row_edges(parts)
    width = own.shape[1]

    def kernel(terms, *rest):
        out, buffer, sems = rest[-3:]
        parity = lax.axis_index("frame") % 2
        frame = parity if role == "E" else 1 - parity
        copies = []
        for part in range(parts):
            start, rows = edges[part], edges[part + 1] - edges[part]
            span = slice(start, start + rows)
            buffer[span, :] = (terms[span, :] + rest[part][...].astype(F32)).astype(BF16)
            copies.append(
                pltpu.make_async_copy(
                    buffer.at[pl.ds(start, rows)],
                    out.at[pl.ds(pl.multiple_of(frame * FRAME_TOK + start, 16), rows)],
                    sems.at[part],
                )
            )
            copies[-1].start()
        for copy in copies:
            copy.wait()

    operands = [own, *received]
    in_specs = [VMEM] * len(operands)
    aliases = {}
    if into is not None:
        aliases = {len(operands): 0}
        operands.append(into)
        in_specs.append(HBM)
    return pl.pallas_call(
        kernel,
        out_shape=jax.ShapeDtypeStruct((frames_here * FRAME_TOK, width), BF16),
        in_specs=in_specs,
        out_specs=HBM,
        scratch_shapes=[pltpu.VMEM((FRAME_TOK, width), BF16), pltpu.SemaphoreType.DMA((parts,))],
        input_output_aliases=aliases,
        compiler_params=params(),
    )(*operands)


def body(query_tok, key_tok, value_tok, head_span, out_weight):
    frames = lax.axis_size("frame")
    groups = lax.axis_size("head")
    local_frames = key_tok.shape[0] // FRAME_TOK
    bits = groups.bit_length() - 1
    assert local_frames == 2 and frames % 2 == 0 and groups == 1 << bits and FRAME_TOK % bits == 0

    def swap(value):
        return lax.ppermute(value, "frame", [(i, i ^ 1) for i in range(frames)])

    def across(value):
        pairs = [(i, i + 1) for i in range(1, frames - 1, 2)]
        return lax.ppermute(value, "frame", pairs + [(b, a) for a, b in pairs])

    edge = pack_frame(key_tok, value_tok, True)
    inner = pack_frame(key_tok, value_tok, False)
    near = across(edge)
    partner_inner = swap(inner)
    partner_edge = swap(edge)
    second = across(inner)
    third = across(partner_inner)
    state = attend_chip(head_span, query_tok, edge, inner, partner_inner, partner_edge)
    beyond = swap(near)
    state = attend_near(head_span, query_tok, state, near)
    state, attended = attend_beyond(head_span, query_tok, state, beyond)
    attended["I"] = attend_inner(head_span, query_tok, state["I"], second, attended["I"])

    def exchange(value, stage, part):
        pairs = []
        for head in range(groups):
            for place in range(frames):
                other = head ^ (1 << mesh_bit(stage, part, place % 2, bits))
                pairs.append((head * frames + place, other * frames + place))
        return lax.ppermute(value, ("head", "frame"), pairs)

    held = {role: [list(range(groups)) for _ in range(bits)] for role in "IE"}
    received = {role: [[] for _ in range(bits)] for role in "IE"}

    def gathered(role, part, slots):
        return [(array, [kept.index(s) for s in slots]) for array, kept in received[role][part]]

    def halve(role, stage):
        for part in range(bits):
            sent = [s for s in held[role][part] if s >> stage & 1]
            kept = [s for s in held[role][part] if not s >> stage & 1]
            terms = project(attended[role], part, bits, out_weight, sent, gathered(role, part, sent))
            received[role][part].append((exchange(terms, stage, part), kept))
            held[role][part] = kept

    halve("I", 0)
    state_e, attended["E"] = attend_edge(head_span, query_tok, state["E"], second, attended["E"])
    attended["E"] = attend_last(head_span, query_tok, state_e, third, attended["E"])
    for stage in range(bits):
        halve("E", stage)
        if stage + 1 < bits:
            halve("I", stage + 1)
    result = None
    for role in "IE":
        terms = [gathered(role, part, [0]) for part in range(bits)]
        own = sum_own(attended[role], bits, out_weight, [t[:-1] for t in terms])
        result = finish(role, own, [t[-1][0] for t in terms], local_frames, result)
    return result


def solution(mesh):
    return jax.shard_map(
        body,
        mesh=mesh,
        in_specs=(
            P("frame", "head"),
            P("frame", "head"),
            P("frame", "head"),
            P("head"),
            P("head", None),
        ),
        out_specs=P("frame", "head"),
        check_vma=False,
    )
```
